512 devices in a mesh: blk: 32 (over y, z_lo, core), rep: 16 (over x, z_hi).
Axes of the slice: x: 4, y: 4, z: 16 (z_hi: 4, z_lo: 4; z = z_hi * 4 + z_lo), core: 2. Of those that a mesh axis runs over, the one named last changes fastest.
Arguments:
- point_pool: bfloat16 [655360, 1024], P(('blk', 'rep')), may hold values from -8 to 8
- batch_rows: int32 [524288], P(('blk', 'rep')), may hold values from 0 to 1279
- targets: bfloat16 [524288, 256], P(('blk', 'rep')), may hold values from -6 to 6
- center_pool: bfloat16 [2048, 1024], P('blk'), may hold values from -8 to 8
- center_rows: int32 [1024], P('blk'), may hold values from 0 to 63
- coefs: bfloat16 [1024, 256], P('blk'), may hold values from -1.5 to 1.5
Outputs:
- residual: float32 [524288, 256], P(('blk', 'rep'))
- coef_grad: float32 [1024, 256], P('blk')
The draws below stay inside these ranges and needn't reach their ends.
All inputs are finite; a program needn't handle non-finite values.
Results may differ from the reference program's by a relative error of at most 0.0016.
Values may be sent and summed in bfloat16 or wider, within the bound.
A program may use at most 64 MiB of HBM per device.

```python
import jax
import jax.numpy as jnp
from jax import lax

D = 1024
OUTS = 256
PTS_DEV = 1024
CEN_DEV = 32
POOL_DEV = 1280
CPOOL_DEV = 64
POINTS = 524288
POOL = 655360
CENTERS = 1024
CPOOL = 2048


def shared_rows(key, row_count, stream_id):
    latent_dims = 16
    mixing = jax.random.normal(jax.random.fold_in(key, 101), (latent_dims, D), jnp.float32)
    spread = 0.245
    jitter = 0.3 * jax.random.normal(jax.random.fold_in(key, stream_id + 1), (row_count, D), jnp.float32)
    latent = spread * jax.random.normal(jax.random.fold_in(key, stream_id), (row_count, latent_dims), jnp.float32)
    result_rows = jnp.dot(latent, mixing, precision=lax.Precision.HIGHEST) + jitter
    return jnp.clip(result_rows, -8.0, 8.0)


def draw_point_pool(key, part):
    return shared_rows(key, POOL, 211).astype(jnp.bfloat16)


def draw_center_pool(key, part):
    return shared_rows(key, CPOOL, 307).astype(jnp.bfloat16)


def draw_targets(key, part):
    block_count = POINTS // PTS_DEV
    shifts = jax.random.uniform(jax.random.fold_in(key, 401), (block_count, 1, 1), jnp.float32, 0.0, 3.0)
    noise = jax.random.normal(jax.random.fold_in(key, 405), (block_count, PTS_DEV, OUTS), jnp.float32)
    values = jnp.clip(noise + shifts, -6.0, 6.0)
    return values.reshape(POINTS, OUTS).astype(jnp.bfloat16)


def touch_ends(result, key, smallest, largest):
    extent = result.shape
    place = [jax.random.randint(jax.random.fold_in(key, axis), (), 0, extent[axis]) for axis in range(len(extent))]
    result = result.at[tuple(place)].set(smallest)
    longest = extent.index(max(extent))
    place[longest] = (place[longest] + 1) % extent[longest]
    return result.at[tuple(place)].set(largest)


def steps_of(key, shape, split, low, top_value):
    factor_of = 1.0
    for dim, blocks in split:
        draws = jax.random.uniform(jax.random.fold_in(jax.random.fold_in(key, 6), dim), (blocks,), jnp.float32, low / len(split), top_value / len(split))
        factor_of = factor_of * jnp.repeat(jnp.exp(draws), shape[dim] // blocks).reshape((-1,) + (1,) * (len(shape) - 1 - dim))
    return factor_of


def scatter_about(stream_key, dims, scale, most, cuts=(), kind=jnp.bfloat16):
    gain = steps_of(stream_key, dims, cuts, -0.22, 0.18) if cuts else 1.0
    values = jax.random.normal(stream_key, dims, jnp.float32) * scale * gain
    return jnp.minimum(jnp.maximum(values, -most), most).astype(kind)


def setup_inputs(seed: int = 0) -> dict:
    arg_keys = jax.random.split(jax.random.key(seed), 7)
    point_pool = draw_point_pool(jax.random.fold_in(arg_keys[6], 71), 0)
    batch_rows = touch_ends(jax.random.randint(arg_keys[1], (POINTS,), 0, POOL_DEV), jax.random.fold_in(arg_keys[1], 1), 0, POOL_DEV - 1).astype(jnp.int32)
    targets = draw_targets(jax.random.fold_in(arg_keys[6], 71), 0)
    center_pool = draw_center_pool(jax.random.fold_in(arg_keys[6], 71), 0)
    center_rows = touch_ends(jax.random.randint(arg_keys[4], (CENTERS,), 0, CPOOL_DEV), jax.random.fold_in(arg_keys[4], 1), 0, CPOOL_DEV - 1).astype(jnp.int32)
    coefs = scatter_about(arg_keys[5], (CENTERS, OUTS), (max(CENTERS // 55, 1)) ** -0.5, 1.5, ((0, 32),))
    return {"point_pool": point_pool, "batch_rows": batch_rows, "targets": targets, "center_pool": center_pool, "center_rows": center_rows, "coefs": coefs}


def reference(point_pool, batch_rows, targets, center_pool, center_rows, coefs):
    owner = jnp.arange(POINTS, dtype=jnp.int32) // PTS_DEV
    points = jnp.take(point_pool, (owner * POOL_DEV + batch_rows).astype(jnp.int32), axis=0)
    center_owner = jnp.arange(CENTERS, dtype=jnp.int32) // CEN_DEV
    centers = jnp.take(center_pool, (center_owner * CPOOL_DEV + center_rows).astype(jnp.int32), axis=0)
    center_norm = jnp.sum(centers.astype(jnp.float32) ** 2, axis=1)
    blocks = POINTS // PTS_DEV
    point_blocks = points.reshape(blocks, PTS_DEV, D)
    target_blocks = targets.reshape(blocks, PTS_DEV, OUTS)

    def step(grad_sum, items):
        block_points, block_targets = items
        point_norm = jnp.sum(block_points.astype(jnp.float32) ** 2, axis=1)
        inner = jnp.dot(block_points, centers.T, preferred_element_type=jnp.float32)
        distance = point_norm[:, None] + center_norm[None, :] - 2.0 * inner
        kernel = jnp.exp(-distance / D).astype(jnp.bfloat16)
        prediction = jnp.dot(kernel, coefs, preferred_element_type=jnp.float32)
        block_residual = prediction - block_targets.astype(jnp.float32)
        residual_b = block_residual.astype(jnp.bfloat16)
        grad_sum = grad_sum + jnp.dot(kernel.T, residual_b, preferred_element_type=jnp.float32)
        return grad_sum, block_residual

    grad_init = jnp.zeros((CENTERS, OUTS), jnp.float32)
    coef_grad, residual = lax.scan(step, grad_init, (point_blocks, target_blocks))
    return residual.reshape(POINTS, OUTS), coef_grad
```

```python
import functools

import jax
import jax.numpy as jnp
from jax import lax
from jax.experimental import pallas as pl
from jax.experimental.pallas import tpu as pltpu
from jax.sharding import PartitionSpec as P

MESH = pl.DeviceIdType.MESH
F32 = jnp.float32
BF16 = jnp.bfloat16
OFFS = (0, 1, -1, 2)
NEG = (0, 2, 1, 3)
NX, NY, NL, NH, NZ = 4, 4, 4, 4, 16


def place():
    b = lax.axis_index("blk")
    r = lax.axis_index("rep")
    core = b % 2
    return (r // NH, b // (2 * NL), (r % NH) * NL + (b // 2) % NL, core)


def at(here, f=0, s=0, x=0, z=0, partner=False):
    px, py, pz, core = here
    nx = (px + x + NX) % NX
    ny = (py + (1 - core) * f + core * s + NY) % NY
    nz = (pz + core * f + (1 - core) * s + z + NZ) % NZ
    nc = 1 - core if partner else core
    return {"blk": (ny * NL + nz % NL) * 2 + nc, "rep": nx * NH + nz // NL}


def fx_offset(i, j):
    df = OFFS[i]
    if df == 2 and j in (1, 2):
        df = -2
    return df, OFFS[j]


def destinations():
    out = [dict(partner=True)]
    for k in (1, -1, 2, -2):
        out += [dict(f=k), dict(s=k)]
    for k in (1, -1, 2):
        out.append(dict(x=k))
    for i in (1, 2, 3):
        for j in (1, 2, 3):
            df, dx = fx_offset(i, j)
            out.append(dict(f=df, x=dx))
    for k in (4, -4, 8):
        out.append(dict(z=k))
    return out


def opposite(offset):
    return {k: (v if k == "partner" else -v) for k, v in offset.items()}


def kernel(
    pool_hbm, rows_ref, targets_hbm, cpool_hbm, crows_ref, coefs_hbm,
    res_hbm, grad_ref,
    cen, pool, sel, pts, pnorm, kern, pred, resb, targ, cpool,
    gq, gq_in, gs, gs_in, gf, gf_in, gz, gz_in, out,
    lsem, send1, send2, send_c, recv_p, recv_q,
    sgq, rgq, sgs, rgs, sgf, rgf, sgz, rgz, sgx, rgx,
):
    here = place()
    npts, d = pts.shape
    npool = pool.shape[0]
    ncen = cen.shape[3]
    outs = pred.shape[1]
    group = 8 * ncen
    half = ncen // 2

    get_cpool = pltpu.make_async_copy(cpool_hbm, cpool, lsem.at[0])
    get_coefs = pltpu.make_async_copy(coefs_hbm, cen.at[0, 0, 0, :, pl.ds(d, outs)], lsem.at[1])
    get_pool = pltpu.make_async_copy(pool_hbm, pool, lsem.at[2])
    get_targ = pltpu.make_async_copy(targets_hbm, targ, lsem.at[3])
    get_cpool.start()
    get_coefs.start()
    get_pool.start()
    get_targ.start()

    barrier = pltpu.get_barrier_semaphore()
    dests = destinations()
    for offset in dests:
        pl.semaphore_signal(barrier, inc=1, device_id=at(here, **opposite(offset)), device_id_type=MESH)

    pending = []

    def send(src, dst, ssem, rsem, **offset):
        copy = pltpu.make_async_remote_copy(
            src_ref=src, dst_ref=dst, send_sem=ssem, recv_sem=rsem,
            device_id=at(here, **offset), device_id_type=MESH,
        )
        copy.start()
        pending.append(copy)

    def arrived(ref, rsem):
        pltpu.make_async_remote_copy(
            src_ref=ref, dst_ref=ref, send_sem=sgx.at[0], recv_sem=rsem,
            device_id=at(here, partner=True), device_id_type=MESH,
        ).wait_recv()

    get_cpool.wait()
    chosen = (
        lax.broadcasted_iota(jnp.int32, (cpool.shape[0], ncen), 0) == crows_ref[...]
    ).astype(F32).astype(BF16)
    cen[0, 0, 0, :, 0:d] = lax.dot_general(
        chosen, cpool[...], (((0,), (0,)), ((), ())), preferred_element_type=F32
    ).astype(BF16)

    def select_chunk(k, _):
        row = jnp.broadcast_to(rows_ref[pl.ds(k, 1), :].astype(F32), (128, 128))
        col = jnp.concatenate([row.T.astype(jnp.int32)] * (npool // 128), axis=1)
        hit = col == lax.broadcasted_iota(jnp.int32, (128, npool), 1)
        sel[pl.ds(pl.multiple_of(k * 128, 128), 128), :] = hit.astype(F32).astype(BF16)
        return 0

    lax.fori_loop(0, npts // 128, select_chunk, 0)
    get_coefs.wait()
    pl.semaphore_wait(barrier, len(dests))

    def spread_first():
        block = cen.at[0, 0, 0]
        for i in (1, 2):
            send(block, cen.at[0, 0, NEG[i]], send1.at[i], recv_p.at[0, NEG[i]], f=OFFS[i])
        send(block.at[0:half], cen.at[0, 0, 3, 0:half], send1.at[0], recv_p.at[0, 3], f=2)
        send(block.at[half:ncen], cen.at[0, 0, 3, half:ncen], send1.at[3], recv_p.at[0, 3], f=-2)

    def spread_second(i):
        block = cen.at[0, 0, i]
        for j in (1, 2):
            send(block, cen.at[NEG[j], 0, i], send2.at[i, j], recv_p.at[NEG[j], i], s=OFFS[j])
        send(block.at[0:half], cen.at[3, 0, i, 0:half], send2.at[i, 0], recv_p.at[3, i], s=2)
        send(block.at[half:ncen], cen.at[3, 0, i, half:ncen], send2.at[i, 3], recv_p.at[3, i], s=-2)

    def share(j, i):
        send(cen.at[j, 0, i], cen.at[j, 1, i], send_c.at[j, i], recv_q.at[j, i], partner=True)

    spread_first()
    spread_second(0)
    share(0, 0)

    get_pool.wait()

    def gather_chunk(n, _):
        cols = pl.ds(pl.multiple_of(n * 256, 256), 256)
        got = jnp.dot(sel[...], pool[:, cols], preferred_element_type=F32)
        pts[:, cols] = got.astype(BF16)
        square = jnp.sum(got * got, axis=1, keepdims=True)

        @pl.when(n == 0)
        def _():
            pnorm[...] = square

        @pl.when(n > 0)
        def _():
            pnorm[...] += square

        return 0

    lax.fori_loop(0, d // 256, gather_chunk, 0)

    for i in (1, 2, 3):
        arrived(cen.at[0, 0, i], recv_p.at[0, i])
        spread_second(i)
        share(0, i)

    get_targ.wait()

    def group_work(j):
        centers = cen[j, :, :, :, 0:d].reshape(group, d)
        weights = cen[j, :, :, :, d : d + outs].reshape(group, outs)
        square = centers.astype(F32)
        square = square * square
        part = square[:, 0:128]
        for t in range(1, d // 128):
            part = part + square[:, t * 128 : (t + 1) * 128]
        cnorm = jnp.sum(part.T, axis=0, keepdims=True)
        step = npts // 4

        def rows_work(r, _):
            rows = pl.ds(pl.multiple_of(r * step, step), step)
            inner = lax.dot_general(
                pts[rows, :], centers, (((1,), (1,)), ((), ())), preferred_element_type=F32
            )
            distance = pnorm[rows, :] + cnorm - 2.0 * inner
            block = jnp.exp(distance * (-1.0 / d)).astype(BF16)
            kern[rows, j * group : (j + 1) * group] = block
            term = jnp.dot(block, weights, preferred_element_type=F32)
            if j == 0:
                pred[rows, :] = term - targ[rows, :].astype(F32)
            else:
                pred[rows, :] += term
            return 0

        lax.fori_loop(0, 4, rows_work, 0)

    for j in range(4):
        if j:
            for i in range(4):
                arrived(cen.at[j, 0, i], recv_p.at[j, i])
                share(j, i)
        for i in range(4):
            arrived(cen.at[j, 1, i], recv_q.at[j, i])
        group_work(j)

    put_res = pltpu.make_async_copy(pred, res_hbm, lsem.at[0])
    put_res.start()
    resb[...] = pred[...].astype(BF16)

    def grad_of(j, parity):
        first = j * group + parity * (group // 2)
        return lax.dot_general(
            kern[:, first : first + group // 2], resb[...], (((0,), (0,)), ((), ())),
            preferred_element_type=F32,
        )

    quarter = group // 4
    order = (3, 1, 2, 0)
    for j in order:
        gq[j] = grad_of(j, 1)
        send(gq.at[j], gq_in.at[j], sgq.at[j], rgq.at[j], partner=True)
    for j in order:
        mine = grad_of(j, 0)
        arrived(gq_in.at[j], rgq.at[j])
        both = mine + gq_in[j]
        if j:
            gs[j] = both.astype(BF16)
            if j == 3:
                send(gs.at[3, 0:quarter], gs_in.at[3, 0:quarter], sgs.at[3], rgs.at[3], s=2)
                send(gs.at[3, quarter : 2 * quarter], gs_in.at[3, quarter : 2 * quarter], sgs.at[0], rgs.at[3], s=-2)
            else:
                send(gs.at[j], gs_in.at[NEG[j]], sgs.at[j], rgs.at[NEG[j]], s=OFFS[j])
        else:
            total = both
    for j in (1, 2, 3):
        arrived(gs_in.at[j], rgs.at[j])
        total = total + gs_in[j].astype(F32)
    gf[...] = total.reshape(gf.shape)

    eighth = gf.shape[2]
    for i in range(4):
        for k in range(4):
            if i or k:
                df, dx = fx_offset(i, k)
                piece = (here[0] + dx + NX) % NX
                send(gf.at[i, piece], gf_in.at[NEG[i], NEG[k]], sgf.at[i, k], rgf.at[NEG[i], NEG[k]], f=df, x=dx)
    mine = gf[0, here[0]]
    for i in range(4):
        for k in range(4):
            if i or k:
                arrived(gf_in.at[i, k], rgf.at[i, k])
                mine = mine + gf_in[i, k]

    gz[...] = mine
    for k, dz in enumerate((4, -4, 8)):
        send(gz, gz_in.at[k], sgz.at[k], rgz.at[k], z=dz)
    for k in range(3):
        arrived(gz_in.at[k], rgz.at[k])
    out[here[0]] = (mine + gz_in[0]) + (gz_in[1] + gz_in[2])
    for k in (1, 2, 3):
        send(out.at[here[0]], out.at[here[0]], sgx.at[k], rgx.at[NEG[k]], x=OFFS[k])
    for k in (1, 2, 3):
        arrived(out.at[(here[0] + OFFS[k] + NX) % NX], rgx.at[k])
    grad_ref[...] = out[...].reshape(grad_ref.shape)

    for copy in pending:
        copy.wait_send()
    put_res.wait()


def per_device(point_pool, batch_rows, targets, center_pool, center_rows, coefs):
    npool, d = point_pool.shape
    npts, outs = targets.shape
    ncen = coefs.shape[0]
    vmem = pl.BlockSpec(memory_space=pltpu.VMEM)
    anys = pl.BlockSpec(memory_space=pl.ANY)
    dma = pltpu.SemaphoreType.DMA
    half = 4 * ncen
    sub = ncen // NX
    scratch = [
        pltpu.VMEM((4, 2, 4, ncen, d + outs), BF16),
        pltpu.VMEM((npool, d), BF16),
        pltpu.VMEM((npts, npool), BF16),
        pltpu.VMEM((npts, d), BF16),
        pltpu.VMEM((npts, 1), F32),
        pltpu.VMEM((npts, 32 * ncen), BF16),
        pltpu.VMEM((npts, outs), F32),
        pltpu.VMEM((npts, outs), BF16),
        pltpu.VMEM((npts, outs), BF16),
        pltpu.VMEM(center_pool.shape, BF16),
        pltpu.VMEM((4, half, outs), F32),
        pltpu.VMEM((4, half, outs), F32),
        pltpu.VMEM((4, half, outs), BF16),
        pltpu.VMEM((4, half, outs), BF16),
        pltpu.VMEM((4, NX, sub, outs), F32),
        pltpu.VMEM((4, NX, sub, outs), F32),
        pltpu.VMEM((sub, outs), F32),
        pltpu.VMEM((3, sub, outs), F32),
        pltpu.VMEM((NX, sub, outs), F32),
        dma((4,)), dma((4,)), dma((4, 4)), dma((4, 4)), dma((4, 4)), dma((4, 4)),
        dma((4,)), dma((4,)), dma((4,)), dma((4,)), dma((4, 4)), dma((4, 4)),
        dma((3,)), dma((3,)), dma((4,)), dma((4,)),
    ]
    return pl.pallas_call(
        kernel,
        out_shape=(
            jax.ShapeDtypeStruct((npts, outs), F32),
            jax.ShapeDtypeStruct((ncen, outs), F32),
        ),
        in_specs=[anys, vmem, anys, anys, vmem, anys],
        out_specs=(anys, vmem),
        scratch_shapes=scratch,
        compiler_params=pltpu.CompilerParams(
            collective_id=0, has_side_effects=True, vmem_limit_bytes=56 << 20
        ),
        name="regression",
    )(
        point_pool, batch_rows.reshape(-1, 128), targets, center_pool,
        center_rows.reshape(1, -1), coefs,
    )


def solution(mesh):
    both = ("blk", "rep")
    in_specs = (P(both, None), P(both), P(both, None), P("blk", None), P("blk"), P("blk", None))
    out_specs = (P(both, None), P("blk", None))
    return jax.shard_map(per_device, mesh=mesh, in_specs=in_specs, out_specs=out_specs, check_vma=False)
```

```python
import functools

import jax
import jax.numpy as jnp
from jax import lax
from jax.experimental import pallas as pl
from jax.experimental.pallas import tpu as pltpu
from jax.sharding import PartitionSpec as P

MESH = pl.DeviceIdType.MESH
F32 = jnp.float32
BF16 = jnp.bfloat16
OFFS = (0, 1, -1, 2)
NEG = (0, 2, 1, 3)
NX, NY, NL, NH, NZ = 4, 4, 4, 4, 16
STEPS = 1
S_STAGE = True
SF = ()
KT = True


def place():
    b = lax.axis_index("blk")
    r = lax.axis_index("rep")
    core = lax.rem(b, 2)
    z = lax.rem(r, NH) * NL + lax.rem(lax.div(b, 2), NL)
    return (lax.div(r, NH), lax.div(b, 2 * NL), z, core)


def at(here, f=0, s=0, x=0, z=0, partner=False):
    px, py, pz, core = here
    nx = lax.rem(px + (x + NX), NX)
    ny = lax.rem(py + (1 - core) * f + core * s + NY, NY)
    nz = lax.rem(pz + core * f + (1 - core) * s + (z + NZ), NZ)
    nc = 1 - core if partner else core
    return {"blk": (ny * NL + lax.rem(nz, NL)) * 2 + nc, "rep": nx * NH + lax.div(nz, NL)}


def fx_offset(i, j):
    df = OFFS[i]
    if df == 2 and j in (1, 2):
        df = -2
    return df, OFFS[j]


def destinations():
    out = [dict(partner=True)]
    for k in (1, -1, 2, -2):
        out += [dict(f=k), dict(s=k)]
    for k in (1, -1, 2):
        out.append(dict(x=k))
    return out


def opposite(offset):
    return {k: (v if k == "partner" else -v) for k, v in offset.items()}


def kernel(
    pool_hbm, rows_ref, targ, cpool, crows_ref, coefs_ref,
    res, grad_ref,
    cen, pool, sel, pts, pnorm, kern, resb,
    gq, gq_in, gs, gs_in, gf, gf_in, gz, gz_in, out,
    lsem, send1, send2, send_c, recv_p, recv_q,
    sgq, rgq, sgs, rgs, sgf, rgf, sgz, rgz, sgx, rgx, relay,
):
    npts, d = pts.shape
    npool = pool.shape[0]
    ncen, outs = coefs_ref.shape
    group = 8 * ncen
    half = ncen // 2

    get_pool = pltpu.make_async_copy(pool_hbm, pool, lsem.at[0])
    get_pool.start()

    here = place()
    known = {}

    def device(**offset):
        key = tuple(sorted(offset.items()))
        if key not in known:
            known[key] = at(here, **offset)
        return known[key]

    barrier = pltpu.get_barrier_semaphore()
    dests = destinations()
    for offset in dests:
        pl.semaphore_signal(barrier, inc=1, device_id=device(**opposite(offset)), device_id_type=MESH)

    pending = []

    def send(src, dst, ssem, rsem, **offset):
        copy = pltpu.make_async_remote_copy(
            src_ref=src, dst_ref=dst, send_sem=ssem, recv_sem=rsem,
            device_id=device(**offset), device_id_type=MESH,
        )
        copy.start()
        pending.append(copy)


    def arrived(ref, rsem):
        pltpu.make_async_remote_copy(
            src_ref=ref, dst_ref=ref, send_sem=sgx.at[0], recv_sem=rsem,
            device_id=device(partner=True), device_id_type=MESH,
        ).wait_recv()

    chosen = (
        lax.broadcasted_iota(jnp.int32, (cpool.shape[0], ncen), 0) == crows_ref[...]
    ).astype(F32).astype(BF16)
    cen[0, 0, :, 0:d] = lax.dot_general(
        chosen, cpool[...], (((0,), (0,)), ((), ())), preferred_element_type=F32
    ).astype(BF16)
    cen[0, 0, :, d : d + outs] = coefs_ref[...]

    def select_chunk(k, _):
        row = jnp.broadcast_to(rows_ref[pl.ds(k, 1), :].astype(F32), (128, 128))
        col = jnp.concatenate([row.T.astype(jnp.int32)] * (npool // 128), axis=1)
        hit = col == lax.broadcasted_iota(jnp.int32, (128, npool), 1)
        sel[pl.ds(pl.multiple_of(k * 128, 128), 128), :] = hit.astype(F32).astype(BF16)
        return 0

    pl.semaphore_wait(barrier, len(dests))

    def signal_relay(k, **offset):
        pl.semaphore_signal(relay.at[k], inc=1, device_id=device(**offset), device_id_type=MESH)

    own = (0, 2, 3, 6)
    other = (1, 4, 5, 7)

    def spread_first():
        block = cen.at[0, 0]
        send(block.at[0:half], cen.at[own[3], 0, 0:half], send1.at[0], recv_p.at[3, 0], f=2)
        send(block.at[half:ncen], cen.at[own[3], 0, half:ncen], send1.at[3], recv_p.at[3, 0], f=-2)
        for i in (1, 2):
            send(block, cen.at[own[NEG[i]], 0], send1.at[i], recv_p.at[NEG[i], 0], f=OFFS[i])

    def spread_second(i):
        block = cen.at[own[i], 0]
        if i not in SF:
            send(block.at[0:half], cen.at[own[i], 3, 0:half], send2.at[i, 0], recv_p.at[i, 3], s=2)
            send(block.at[half:ncen], cen.at[own[i], 3, half:ncen], send2.at[i, 3], recv_p.at[i, 3], s=-2)
        for j in (1, 2):
            send(block, cen.at[own[i], NEG[j]], send2.at[i, j], recv_p.at[i, NEG[j]], s=OFFS[j])

    def take(i, j):
        if i or j:
            arrived(cen.at[own[i], j], recv_p.at[i, j])
        if i in SF and j == 1:
            rows = slice(0, half)
            send(cen.at[own[i], 1, rows], cen.at[own[i], 3, rows], send2.at[i, 0], recv_p.at[i, 3], s=-1)
        if i in SF and j == 2:
            rows = slice(half, ncen)
            send(cen.at[own[i], 2, rows], cen.at[own[i], 3, rows], send2.at[i, 3], recv_p.at[i, 3], s=1)
        send(cen.at[own[i], j], cen.at[other[i], j], send_c.at[i, j], recv_q.at[i, j], partner=True)

    def take_other(i):
        for j in range(4):
            arrived(cen.at[other[i], j], recv_q.at[i, j])

    def gather_chunk(n):
        cols = slice(n * 256, n * 256 + 256)
        got = jnp.dot(sel[...], pool[:, cols], preferred_element_type=F32)
        pts[:, cols] = got.astype(BF16)
        square = jnp.sum(got * got, axis=1, keepdims=True)
        if n == 0:
            pnorm[...] = square
        else:
            pnorm[...] += square

    def group_work(g):
        centers = cen[2 * g : 2 * g + 2, :, :, 0:d].reshape(group, d)
        weights = cen[2 * g : 2 * g + 2, :, :, d : d + outs].reshape(group, outs)
        square = centers.astype(F32)
        square = square * square
        part = square[:, 0:128]
        for t in range(1, d // 128):
            part = part + square[:, t * 128 : (t + 1) * 128]
        cnorm = jnp.sum(part.T, axis=0, keepdims=True)
        step = npts // STEPS

        def rows_work(r, _):
            rows = pl.ds(pl.multiple_of(r * step, step), step)
            inner = lax.dot_general(
                pts[rows, :], centers, (((1,), (1,)), ((), ())), preferred_element_type=F32
            )
            distance = pnorm[rows, :] + cnorm - 2.0 * inner
            block = jnp.exp(distance * (-1.0 / d)).astype(BF16)
            if KT:
                kern[g * group : (g + 1) * group, rows] = block.T
            else:
                kern[rows, g * group : (g + 1) * group] = block
            term = jnp.dot(block, weights, preferred_element_type=F32)
            if g == 0:
                res[rows, :] = term - targ[rows, :].astype(F32)
            elif g < 3:
                res[rows, :] += term
            else:
                last = res[rows, :] + term
                res[rows, :] = last
                resb[rows, :] = last.astype(BF16)
            return 0

        lax.fori_loop(0, STEPS, rows_work, 0)

    spread_first()
    take(0, 0)
    for k in (1, -1, 2, -2):
        signal_relay(0, f=k)
    for k in (2, -2):
        signal_relay(0, s=k)
    lax.fori_loop(0, npts // 128, select_chunk, 0)
    spread_second(0)
    get_pool.wait()
    gather_chunk(0)
    gather_chunk(1)
    take(1, 0)
    spread_second(1)
    take(2, 0)
    spread_second(2)
    gather_chunk(2)
    take(3, 0)
    spread_second(3)
    take(0, 1)
    take(0, 2)
    gather_chunk(3)
    pl.semaphore_wait(relay.at[0], 6)
    signal_relay(1, z=4)
    signal_relay(1, z=-4)
    take(0, 3)
    take(1, 1)
    take(1, 2)
    take_other(0)
    group_work(0)
    take(2, 1)
    take(2, 2)
    take(3, 1)
    take(3, 2)
    take(1, 3)
    take(2, 3)
    group_work(1)
    take(3, 3)
    take_other(1)
    take_other(2)
    group_work(2)
    take_other(3)
    group_work(3)
    pl.semaphore_wait(relay.at[1], 2)

    def grad_of(slot):
        part = slice(slot * 4 * ncen, (slot + 1) * 4 * ncen)
        if KT:
            return jnp.dot(kern[part, :], resb[...], preferred_element_type=F32)
        return lax.dot_general(
            kern[:, part], resb[...], (((0,), (0,)), ((), ())), preferred_element_type=F32
        )

    for i in range(4):
        gq[i] = grad_of(other[i])
        send(gq.at[i], gq_in.at[i], sgq.at[i], rgq.at[i], partner=True)
    total = []
    for i in range(4):
        mine = grad_of(own[i])
        arrived(gq_in.at[i], rgq.at[i])
        both = mine + gq_in[i]
        total.append(both[0:ncen])
        for j in (1, 2, 3):
            gs[j, i] = both[j * ncen : (j + 1) * ncen].astype(BF16)
        if S_STAGE and i == 1:
            send(gs.at[3, 0:2], gs_in.at[3, 0:2], sgs.at[3], rgs.at[3], s=2)
        if S_STAGE and i == 3:
            send(gs.at[3, 2:4], gs_in.at[3, 2:4], sgs.at[0], rgs.at[3], s=-2)
            for j in (1, 2):
                send(gs.at[j], gs_in.at[NEG[j]], sgs.at[j], rgs.at[NEG[j]], s=OFFS[j])
    for j in (1, 2, 3):
        arrived(gs_in.at[j], rgs.at[j])
    eighth = ncen // NX
    for i in (3, 1, 2, 0):
        whole = total[i] + gs_in[1, i].astype(F32) + gs_in[2, i].astype(F32) + gs_in[3, i].astype(F32)
        gf[i] = whole.reshape(NX, eighth, outs)
    for i in (3, 1, 2, 0):
        for k in (3, 1, 2, 0):
            if i or k:
                df, dx = fx_offset(i, k)
                piece = lax.rem(here[0] + (dx + NX), NX)
                send(gf.at[i, piece], gf_in.at[NEG[i], NEG[k]], sgf.at[i, k], rgf.at[NEG[i], NEG[k]], f=df, x=dx)
    mine = gf[0, here[0]]
    for i in range(4):
        for k in range(4):
            if i or k:
                arrived(gf_in.at[i, k], rgf.at[i, k])
                mine = mine + gf_in[i, k]

    gz[...] = mine
    for k, dz in enumerate((4, -4, 8)):
        send(gz, gz_in.at[k], sgz.at[k], rgz.at[k], z=dz)
    for k in range(3):
        arrived(gz_in.at[k], rgz.at[k])
    out[here[0]] = (mine + gz_in[0]) + (gz_in[1] + gz_in[2])
    for k in (3, 1, 2):
        send(out.at[here[0]], out.at[here[0]], sgx.at[k], rgx.at[NEG[k]], x=OFFS[k])
    for k in (1, 2, 3):
        arrived(out.at[lax.rem(here[0] + (OFFS[k] + NX), NX)], rgx.at[k])
    grad_ref[...] = out[...].reshape(grad_ref.shape)

    for copy in pending:
        copy.wait_send()


def per_device(point_pool, batch_rows, targets, center_pool, center_rows, coefs):
    npool, d = point_pool.shape
    npts, outs = targets.shape
    ncen = coefs.shape[0]
    vmem = pl.BlockSpec(memory_space=pltpu.VMEM)
    anys = pl.BlockSpec(memory_space=pl.ANY)
    dma = pltpu.SemaphoreType.DMA
    half = 4 * ncen
    sub = ncen // NX
    scratch = [
        pltpu.VMEM((8, 4, ncen, d + outs), BF16),
        pltpu.VMEM((npool, d), BF16),
        pltpu.VMEM((npts, npool), BF16),
        pltpu.VMEM((npts, d), BF16),
        pltpu.VMEM((npts, 1), F32),
        pltpu.VMEM((npts, 32 * ncen), BF16),
        pltpu.VMEM((npts, outs), BF16),
        pltpu.VMEM((4, half, outs), F32),
        pltpu.VMEM((4, half, outs), F32),
        pltpu.VMEM((4, 4, ncen, outs), BF16),
        pltpu.VMEM((4, 4, ncen, outs), BF16),
        pltpu.VMEM((4, NX, sub, outs), F32),
        pltpu.VMEM((4, NX, sub, outs), F32),
        pltpu.VMEM((sub, outs), F32),
        pltpu.VMEM((3, sub, outs), F32),
        pltpu.VMEM((NX, sub, outs), F32),
        dma((1,)), dma((4,)), dma((4, 4)), dma((4, 4)), dma((4, 4)), dma((4, 4)),
        dma((4,)), dma((4,)), dma((4,)), dma((4,)), dma((4, 4)), dma((4, 4)),
        dma((3,)), dma((3,)), dma((4,)), dma((4,)), pltpu.SemaphoreType.REGULAR((2,)),
    ]
    return pl.pallas_call(
        kernel,
        out_shape=(
            jax.ShapeDtypeStruct((npts, outs), F32),
            jax.ShapeDtypeStruct((ncen, outs), F32),
        ),
        in_specs=[anys, vmem, vmem, vmem, vmem, vmem],
        out_specs=(vmem, vmem),
        scratch_shapes=scratch,
        compiler_params=pltpu.CompilerParams(
            collective_id=0, has_side_effects=True, vmem_limit_bytes=52 << 20
        ),
        name="regression",
    )(
        point_pool, batch_rows.reshape(-1, 128), targets, center_pool,
        center_rows.reshape(1, -1), coefs,
    )


def solution(mesh):
    both = ("blk", "rep")
    in_specs = (P(both, None), P(both), P(both, None), P("blk", None), P("blk"), P("blk", None))
    out_specs = (P(both, None), P("blk", None))
    return jax.shard_map(per_device, mesh=mesh, in_specs=in_specs, out_specs=out_specs, check_vma=False)
```

```python
import functools

import jax
import jax.numpy as jnp
from jax import lax
from jax.experimental import pallas as pl
from jax.experimental.pallas import tpu as pltpu
from jax.sharding import PartitionSpec as P

MESH = pl.DeviceIdType.MESH
F32 = jnp.float32
BF16 = jnp.bfloat16
OFFS = (0, 1, -1, 2)
NEG = (0, 2, 1, 3)
NX, NY, NL, NH, NZ = 4, 4, 4, 4, 16
STEPS = 1
PLAN = (
    ("first",), ("take", 0, 0), ("near",), ("select",), ("second", 0),
    ("gather", 0), ("gather", 1),
    ("take", 1, 0), ("second", 1), ("take", 2, 0), ("second", 2),
    ("gather", 2),
    ("take", 3, 0), ("second", 3), ("take", 0, 1), ("take", 0, 2),
    ("gather", 3), ("far",),
    ("take", 0, 3), ("take", 1, 1), ("take", 1, 2), ("other", 0),
    ("group", 0),
    ("take", 2, 1), ("take", 2, 2), ("take", 3, 1), ("take", 3, 2), ("take", 1, 3), ("take", 2, 3),
    ("group", 1),
    ("take", 3, 3), ("other", 1), ("other", 2),
    ("group", 2),
    ("other", 3),
    ("group", 3),
)


def place():
    b = lax.axis_index("blk")
    r = lax.axis_index("rep")
    core = lax.rem(b, 2)
    z = lax.rem(r, NH) * NL + lax.rem(lax.div(b, 2), NL)
    return (lax.div(r, NH), lax.div(b, 2 * NL), z, core)


def at(here, f=0, s=0, x=0, z=0, partner=False):
    px, py, pz, core = here
    nx = lax.rem(px + (x + NX), NX)
    ny = lax.rem(py + (1 - core) * f + core * s + NY, NY)
    nz = lax.rem(pz + core * f + (1 - core) * s + (z + NZ), NZ)
    nc = 1 - core if partner else core
    return {"blk": (ny * NL + lax.rem(nz, NL)) * 2 + nc, "rep": nx * NH + lax.div(nz, NL)}


def fx_offset(i, j):
    df = OFFS[i]
    if df == 2 and j in (1, 2):
        df = -2
    return df, OFFS[j]


def destinations():
    out = [dict(partner=True)]
    for k in (1, -1, 2, -2):
        out += [dict(f=k), dict(s=k)]
    for k in (1, -1, 2):
        out.append(dict(x=k))
    return out


def opposite(offset):
    return {k: (v if k == "partner" else -v) for k, v in offset.items()}


def kernel(
    pool_hbm, rows_hbm, targ_hbm, cpool_hbm, crows_hbm, coefs_hbm,
    res, grad_ref,
    cen, pool, sel, pts, pnorm, kern, resb, targ, cpool, rows_ref, crows_ref,
    gq, gq_in, gs, gs_in, gf, gf_in, gz, gz_in, out,
    lsem, send1, send2, send_c, recv_p, recv_q,
    sgq, rgq, sgs, rgs, sgf, rgf, sgz, rgz, sgx, rgx, relay,
):
    npts, d = pts.shape
    npool = pool.shape[0]
    ncen, outs = coefs_hbm.shape
    group = 8 * ncen
    half = ncen // 2

    get_crows = pltpu.make_async_copy(crows_hbm, crows_ref, lsem.at[1])
    get_cpool = pltpu.make_async_copy(cpool_hbm, cpool, lsem.at[2])
    get_coefs = pltpu.make_async_copy(coefs_hbm, cen.at[0, 0, :, pl.ds(d, outs)], lsem.at[3])
    get_rows = pltpu.make_async_copy(rows_hbm, rows_ref, lsem.at[4])
    get_pool = pltpu.make_async_copy(pool_hbm, pool, lsem.at[0])
    get_targ = pltpu.make_async_copy(targ_hbm, targ, lsem.at[5])
    for copy in (get_crows, get_cpool, get_coefs, get_rows, get_pool, get_targ):
        copy.start()

    here = place()
    known = {}

    def device(**offset):
        key = tuple(sorted(offset.items()))
        if key not in known:
            known[key] = at(here, **offset)
        return known[key]

    barrier = pltpu.get_barrier_semaphore()
    dests = destinations()
    for offset in dests:
        pl.semaphore_signal(barrier, inc=1, device_id=device(**opposite(offset)), device_id_type=MESH)

    pending = []

    def send(src, dst, ssem, rsem, **offset):
        copy = pltpu.make_async_remote_copy(
            src_ref=src, dst_ref=dst, send_sem=ssem, recv_sem=rsem,
            device_id=device(**offset), device_id_type=MESH,
        )
        copy.start()
        pending.append(copy)


    def arrived(ref, rsem):
        pltpu.make_async_remote_copy(
            src_ref=ref, dst_ref=ref, send_sem=sgx.at[0], recv_sem=rsem,
            device_id=device(partner=True), device_id_type=MESH,
        ).wait_recv()

    get_crows.wait()
    get_cpool.wait()
    chosen = (
        lax.broadcasted_iota(jnp.int32, (cpool.shape[0], ncen), 0) == crows_ref[...]
    ).astype(F32).astype(BF16)
    cen[0, 0, :, 0:d] = lax.dot_general(
        chosen, cpool[...], (((0,), (0,)), ((), ())), preferred_element_type=F32
    ).astype(BF16)
    get_coefs.wait()
    get_rows.wait()
    get_targ.wait()

    def select_chunk(k, _):
        row = jnp.broadcast_to(rows_ref[pl.ds(k, 1), :].astype(F32), (128, 128))
        col = jnp.concatenate([row.T.astype(jnp.int32)] * (npool // 128), axis=1)
        hit = col == lax.broadcasted_iota(jnp.int32, (128, npool), 1)
        sel[pl.ds(pl.multiple_of(k * 128, 128), 128), :] = hit.astype(F32).astype(BF16)
        return 0

    pl.semaphore_wait(barrier, len(dests))

    def signal_relay(k, **offset):
        pl.semaphore_signal(relay.at[k], inc=1, device_id=device(**offset), device_id_type=MESH)

    own = (0, 2, 3, 6)
    other = (1, 4, 5, 7)

    def spread_first():
        block = cen.at[0, 0]
        send(block.at[0:half], cen.at[own[3], 0, 0:half], send1.at[0], recv_p.at[3, 0], f=2)
        send(block.at[half:ncen], cen.at[own[3], 0, half:ncen], send1.at[3], recv_p.at[3, 0], f=-2)
        for i in (1, 2):
            send(block, cen.at[own[NEG[i]], 0], send1.at[i], recv_p.at[NEG[i], 0], f=OFFS[i])

    def spread_second(i):
        block = cen.at[own[i], 0]
        send(block.at[0:half], cen.at[own[i], 3, 0:half], send2.at[i, 0], recv_p.at[i, 3], s=2)
        send(block.at[half:ncen], cen.at[own[i], 3, half:ncen], send2.at[i, 3], recv_p.at[i, 3], s=-2)
        for j in (1, 2):
            send(block, cen.at[own[i], NEG[j]], send2.at[i, j], recv_p.at[i, NEG[j]], s=OFFS[j])

    def take(i, j):
        if i or j:
            arrived(cen.at[own[i], j], recv_p.at[i, j])
        send(cen.at[own[i], j], cen.at[other[i], j], send_c.at[i, j], recv_q.at[i, j], partner=True)

    def take_other(i):
        for j in range(4):
            arrived(cen.at[other[i], j], recv_q.at[i, j])

    def gather_chunk(n):
        cols = slice(n * 256, n * 256 + 256)
        got = jnp.dot(sel[...], pool[:, cols], preferred_element_type=F32)
        pts[:, cols] = got.astype(BF16)
        square = jnp.sum(got * got, axis=1, keepdims=True)
        if n == 0:
            pnorm[...] = square
        else:
            pnorm[...] += square

    def group_work(g):
        centers = cen[2 * g : 2 * g + 2, :, :, 0:d].reshape(group, d)
        weights = cen[2 * g : 2 * g + 2, :, :, d : d + outs].reshape(group, outs)
        square = centers.astype(F32)
        square = square * square
        part = square[:, 0:128]
        for t in range(1, d // 128):
            part = part + square[:, t * 128 : (t + 1) * 128]
        cnorm = jnp.sum(part.T, axis=0, keepdims=True)
        step = npts // STEPS

        def rows_work(r, _):
            rows = pl.ds(pl.multiple_of(r * step, step), step)
            inner = lax.dot_general(
                pts[rows, :], centers, (((1,), (1,)), ((), ())), preferred_element_type=F32
            )
            distance = pnorm[rows, :] + cnorm - 2.0 * inner
            block = jnp.exp(distance * (-1.0 / d)).astype(BF16)
            kern[g * group : (g + 1) * group, rows] = block.T
            term = jnp.dot(block, weights, preferred_element_type=F32)
            if g == 0:
                res[rows, :] = term - targ[rows, :].astype(F32)
            elif g < 3:
                res[rows, :] += term
            else:
                last = res[rows, :] + term
                res[rows, :] = last
                resb[rows, :] = last.astype(BF16)
            return 0

        lax.fori_loop(0, STEPS, rows_work, 0)

    def relay_near():
        for k in (1, -1, 2, -2):
            signal_relay(0, f=k)
        for k in (2, -2):
            signal_relay(0, s=k)

    def relay_far():
        pl.semaphore_wait(relay.at[0], 6)
        signal_relay(1, z=4)
        signal_relay(1, z=-4)

    def select():
        lax.fori_loop(0, npts // 128, select_chunk, 0)
        get_pool.wait()

    steps = {
        "first": spread_first, "second": spread_second, "take": take, "other": take_other,
        "select": select, "gather": gather_chunk, "group": group_work,
        "near": relay_near, "far": relay_far,
    }
    for name, *where in PLAN:
        steps[name](*where)
    pl.semaphore_wait(relay.at[1], 2)

    def grad_of(slot):
        part = slice(slot * 4 * ncen, (slot + 1) * 4 * ncen)
        return jnp.dot(kern[part, :], resb[...], preferred_element_type=F32)

    for i in range(4):
        gq[i] = grad_of(other[i])
        send(gq.at[i], gq_in.at[i], sgq.at[i], rgq.at[i], partner=True)
    total = []
    for i in range(4):
        mine = grad_of(own[i])
        arrived(gq_in.at[i], rgq.at[i])
        both = mine + gq_in[i]
        total.append(both[0:ncen])
        for j in (1, 2, 3):
            gs[j, i] = both[j * ncen : (j + 1) * ncen].astype(BF16)
        if i == 1:
            send(gs.at[3, 0:2], gs_in.at[3, 0:2], sgs.at[3], rgs.at[3], s=2)
        if i == 3:
            send(gs.at[3, 2:4], gs_in.at[3, 2:4], sgs.at[0], rgs.at[3], s=-2)
            for j in (1, 2):
                send(gs.at[j], gs_in.at[NEG[j]], sgs.at[j], rgs.at[NEG[j]], s=OFFS[j])
    for j in (1, 2, 3):
        arrived(gs_in.at[j], rgs.at[j])
    eighth = ncen // NX
    for i in (3, 1, 2, 0):
        whole = total[i] + gs_in[1, i].astype(F32) + gs_in[2, i].astype(F32) + gs_in[3, i].astype(F32)
        gf[i] = whole.reshape(NX, eighth, outs)
    for i in (3, 1, 2, 0):
        for k in (3, 1, 2, 0):
            if i or k:
                df, dx = fx_offset(i, k)
                piece = lax.rem(here[0] + (dx + NX), NX)
                send(gf.at[i, piece], gf_in.at[NEG[i], NEG[k]], sgf.at[i, k], rgf.at[NEG[i], NEG[k]], f=df, x=dx)
    mine = gf[0, here[0]]
    for i in range(4):
        for k in range(4):
            if i or k:
                arrived(gf_in.at[i, k], rgf.at[i, k])
                mine = mine + gf_in[i, k]

    gz[...] = mine
    for k, dz in enumerate((4, -4, 8)):
        send(gz, gz_in.at[k], sgz.at[k], rgz.at[k], z=dz)
    for k in range(3):
        arrived(gz_in.at[k], rgz.at[k])
    out[here[0]] = (mine + gz_in[0]) + (gz_in[1] + gz_in[2])
    for k in (3, 1, 2):
        send(out.at[here[0]], out.at[here[0]], sgx.at[k], rgx.at[NEG[k]], x=OFFS[k])
    for k in (1, 2, 3):
        arrived(out.at[lax.rem(here[0] + (OFFS[k] + NX), NX)], rgx.at[k])
    grad_ref[...] = out[...].reshape(grad_ref.shape)

    for copy in pending:
        copy.wait_send()


def per_device(point_pool, batch_rows, targets, center_pool, center_rows, coefs):
    batch_rows, center_rows = batch_rows.reshape(-1, 128), center_rows.reshape(1, -1)
    npool, d = point_pool.shape
    npts, outs = targets.shape
    ncen = coefs.shape[0]
    vmem = pl.BlockSpec(memory_space=pltpu.VMEM)
    anys = pl.BlockSpec(memory_space=pl.ANY)
    dma = pltpu.SemaphoreType.DMA
    half = 4 * ncen
    sub = ncen // NX
    scratch = [
        pltpu.VMEM((8, 4, ncen, d + outs), BF16),
        pltpu.VMEM((npool, d), BF16),
        pltpu.VMEM((npts, npool), BF16),
        pltpu.VMEM((npts, d), BF16),
        pltpu.VMEM((npts, 1), F32),
        pltpu.VMEM((npts, 32 * ncen), BF16),
        pltpu.VMEM((npts, outs), BF16),
        pltpu.VMEM((npts, outs), BF16),
        pltpu.VMEM(center_pool.shape, BF16),
        pltpu.VMEM((npts // 128, 128), jnp.int32),
        pltpu.VMEM((1, ncen), jnp.int32),
        pltpu.VMEM((4, half, outs), F32),
        pltpu.VMEM((4, half, outs), F32),
        pltpu.VMEM((4, 4, ncen, outs), BF16),
        pltpu.VMEM((4, 4, ncen, outs), BF16),
        pltpu.VMEM((4, NX, sub, outs), F32),
        pltpu.VMEM((4, NX, sub, outs), F32),
        pltpu.VMEM((sub, outs), F32),
        pltpu.VMEM((3, sub, outs), F32),
        pltpu.VMEM((NX, sub, outs), F32),
        dma((6,)), dma((4,)), dma((4, 4)), dma((4, 4)), dma((4, 4)), dma((4, 4)),
        dma((4,)), dma((4,)), dma((4,)), dma((4,)), dma((4, 4)), dma((4, 4)),
        dma((3,)), dma((3,)), dma((4,)), dma((4,)), pltpu.SemaphoreType.REGULAR((2,)),
    ]
    return pl.pallas_call(
        kernel,
        out_shape=(
            jax.ShapeDtypeStruct((npts, outs), F32),
            jax.ShapeDtypeStruct((ncen, outs), F32),
        ),
        in_specs=[anys] * 6,
        out_specs=(vmem, vmem),
        scratch_shapes=scratch,
        compiler_params=pltpu.CompilerParams(
            collective_id=0, has_side_effects=True, vmem_limit_bytes=44 << 20
        ),
        name="regression",
    )(*(
        pltpu.with_memory_space_constraint(a, pltpu.HBM)
        for a in (point_pool, batch_rows, targets, center_pool, center_rows, coefs)
    ))


def solution(mesh):
    both = ("blk", "rep")
    in_specs = (P(both, None), P(both), P(both, None), P("blk", None), P("blk"), P("blk", None))
    out_specs = (P(both, None), P("blk", None))
    return jax.shard_map(per_device, mesh=mesh, in_specs=in_specs, out_specs=out_specs, check_vma=False)
```

```python
import functools

import jax
import jax.numpy as jnp
from jax import lax
from jax.experimental import pallas as pl
from jax.experimental.pallas import tpu as pltpu
from jax.sharding import PartitionSpec as P

MESH = pl.DeviceIdType.MESH
F32 = jnp.float32
BF16 = jnp.bfloat16
OFFS = (0, 1, -1, 2)
NEG = (0, 2, 1, 3)
NX, NY, NL, NH, NZ = 4, 4, 4, 4, 16
STEPS = 1
PLAN = (
    ("first",), ("take", 0, 0), ("near",), ("select",), ("second", 0),
    ("gather", 0), ("gather", 1),
    ("take", 1, 0), ("second", 1), ("take", 2, 0), ("second", 2),
    ("gather", 2),
    ("take", 3, 0), ("second", 3), ("take", 0, 1), ("take", 0, 2), ("take", 0, 3),
    ("gather", 3), ("far",), ("other", 0),
    ("group", 0),
    ("take", 1, 1), ("take", 1, 2), ("take", 2, 1), ("take", 2, 2), ("take", 1, 3), ("take", 2, 3),
    ("group", 1),
    ("take", 3, 1), ("take", 3, 2), ("take", 3, 3), ("other", 1), ("other", 2),
    ("group", 2),
    ("other", 3),
    ("group", 3),
)


def place():
    b = lax.axis_index("blk")
    r = lax.axis_index("rep")
    core = lax.rem(b, 2)
    z = lax.rem(r, NH) * NL + lax.rem(lax.div(b, 2), NL)
    return (lax.div(r, NH), lax.div(b, 2 * NL), z, core)


def at(here, f=0, s=0, x=0, z=0, partner=False):
    px, py, pz, core = here
    nx = lax.rem(px + (x + NX), NX)
    ny = lax.rem(py + (1 - core) * f + core * s + NY, NY)
    nz = lax.rem(pz + core * f + (1 - core) * s + (z + NZ), NZ)
    nc = 1 - core if partner else core
    return {"blk": (ny * NL + lax.rem(nz, NL)) * 2 + nc, "rep": nx * NH + lax.div(nz, NL)}


def fx_offset(i, j):
    df = OFFS[i]
    if df == 2 and j in (1, 2):
        df = -2
    return df, OFFS[j]


def destinations():
    out = [dict(partner=True)]
    for k in (1, -1, 2, -2):
        out += [dict(f=k), dict(s=k)]
    for k in (1, -1, 2):
        out.append(dict(x=k))
    return out


def opposite(offset):
    return {k: (v if k == "partner" else -v) for k, v in offset.items()}


def kernel(
    pool_hbm, rows_hbm, targ_hbm, cpool_hbm, crows_hbm, coefs_hbm,
    res, grad_ref,
    cen, pool, sel, pts, pnorm, kern, resb, targ, cpool, rows_ref, crows_ref,
    gq, gq_in, gs, gs_in, gf, gf_in, gz, gz_in, out,
    lsem, send1, send2, send_c, recv_p, recv_q,
    sgq, rgq, sgs, rgs, sgf, rgf, sgz, rgz, sgx, rgx, relay,
):
    npts, d = pts.shape
    npool = pool.shape[0]
    ncen, outs = coefs_hbm.shape
    group = 8 * ncen
    half = ncen // 2

    get_crows = pltpu.make_async_copy(crows_hbm, crows_ref, lsem.at[1])
    get_cpool = pltpu.make_async_copy(cpool_hbm, cpool, lsem.at[2])
    get_coefs = pltpu.make_async_copy(coefs_hbm, cen.at[0, 0, :, pl.ds(d, outs)], lsem.at[3])
    get_rows = pltpu.make_async_copy(rows_hbm, rows_ref, lsem.at[4])
    get_pool = pltpu.make_async_copy(pool_hbm, pool, lsem.at[0])
    get_targ = pltpu.make_async_copy(targ_hbm, targ, lsem.at[5])
    for copy in (get_crows, get_cpool, get_coefs, get_rows, get_pool, get_targ):
        copy.start()

    here = place()
    known = {}

    def device(**offset):
        key = tuple(sorted(offset.items()))
        if key not in known:
            known[key] = at(here, **offset)
        return known[key]

    barrier = pltpu.get_barrier_semaphore()
    dests = destinations()
    for offset in dests:
        pl.semaphore_signal(barrier, inc=1, device_id=device(**opposite(offset)), device_id_type=MESH)

    pending = []

    def send(src, dst, ssem, rsem, **offset):
        copy = pltpu.make_async_remote_copy(
            src_ref=src, dst_ref=dst, send_sem=ssem, recv_sem=rsem,
            device_id=device(**offset), device_id_type=MESH,
        )
        copy.start()
        pending.append(copy)


    def arrived(ref, rsem):
        pltpu.make_async_remote_copy(
            src_ref=ref, dst_ref=ref, send_sem=sgx.at[0], recv_sem=rsem,
            device_id=device(partner=True), device_id_type=MESH,
        ).wait_recv()

    get_crows.wait()
    get_cpool.wait()
    chosen = (
        lax.broadcasted_iota(jnp.int32, (cpool.shape[0], ncen), 0) == crows_ref[...]
    ).astype(F32).astype(BF16)
    cen[0, 0, :, 0:d] = lax.dot_general(
        chosen, cpool[...], (((0,), (0,)), ((), ())), preferred_element_type=F32
    ).astype(BF16)
    get_coefs.wait()
    get_rows.wait()
    get_targ.wait()

    def select_chunk(k, _):
        row = jnp.broadcast_to(rows_ref[pl.ds(k, 1), :].astype(F32), (128, 128))
        col = jnp.concatenate([row.T.astype(jnp.int32)] * (npool // 128), axis=1)
        hit = col == lax.broadcasted_iota(jnp.int32, (128, npool), 1)
        sel[pl.ds(pl.multiple_of(k * 128, 128), 128), :] = hit.astype(F32).astype(BF16)
        return 0

    pl.semaphore_wait(barrier, len(dests))

    def signal_relay(k, **offset):
        pl.semaphore_signal(relay.at[k], inc=1, device_id=device(**offset), device_id_type=MESH)

    own = (0, 2, 3, 6)
    other = (1, 4, 5, 7)

    def spread_first():
        block = cen.at[0, 0]
        send(block.at[0:half], cen.at[own[3], 0, 0:half], send1.at[0], recv_p.at[3, 0], f=2)
        send(block.at[half:ncen], cen.at[own[3], 0, half:ncen], send1.at[3], recv_p.at[3, 0], f=-2)
        for i in (1, 2):
            send(block, cen.at[own[NEG[i]], 0], send1.at[i], recv_p.at[NEG[i], 0], f=OFFS[i])

    def spread_second(i):
        block = cen.at[own[i], 0]
        send(block.at[0:half], cen.at[own[i], 3, 0:half], send2.at[i, 0], recv_p.at[i, 3], s=2)
        send(block.at[half:ncen], cen.at[own[i], 3, half:ncen], send2.at[i, 3], recv_p.at[i, 3], s=-2)
        for j in (1, 2):
            send(block, cen.at[own[i], NEG[j]], send2.at[i, j], recv_p.at[i, NEG[j]], s=OFFS[j])

    def take(i, j):
        if i or j:
            arrived(cen.at[own[i], j], recv_p.at[i, j])
        send(cen.at[own[i], j], cen.at[other[i], j], send_c.at[i, j], recv_q.at[i, j], partner=True)

    def take_other(i):
        for j in range(4):
            arrived(cen.at[other[i], j], recv_q.at[i, j])

    def gather_chunk(n):
        cols = slice(n * 256, n * 256 + 256)
        got = jnp.dot(sel[...], pool[:, cols], preferred_element_type=F32)
        pts[:, cols] = got.astype(BF16)
        square = jnp.sum(got * got, axis=1, keepdims=True)
        if n == 0:
            pnorm[...] = square
        else:
            pnorm[...] += square

    def group_work(g):
        centers = cen[2 * g : 2 * g + 2, :, :, 0:d].reshape(group, d)
        weights = cen[2 * g : 2 * g + 2, :, :, d : d + outs].reshape(group, outs)
        square = centers.astype(F32)
        square = square * square
        part = square[:, 0:128]
        for t in range(1, d // 128):
            part = part + square[:, t * 128 : (t + 1) * 128]
        cnorm = jnp.sum(part.T, axis=0, keepdims=True)
        step = npts // STEPS

        def rows_work(r, _):
            rows = pl.ds(pl.multiple_of(r * step, step), step)
            inner = lax.dot_general(
                pts[rows, :], centers, (((1,), (1,)), ((), ())), preferred_element_type=F32
            )
            distance = pnorm[rows, :] + cnorm - 2.0 * inner
            block = jnp.exp(distance * (-1.0 / d)).astype(BF16)
            kern[g * group : (g + 1) * group, rows] = block.T
            term = jnp.dot(block, weights, preferred_element_type=F32)
            if g == 0:
                res[rows, :] = term - targ[rows, :].astype(F32)
            elif g < 3:
                res[rows, :] += term
            else:
                last = res[rows, :] + term
                res[rows, :] = last
                resb[rows, :] = last.astype(BF16)
            return 0

        lax.fori_loop(0, STEPS, rows_work, 0)

    def relay_near():
        for k in (1, -1, 2, -2):
            signal_relay(0, f=k)
        for k in (2, -2):
            signal_relay(0, s=k)

    def relay_far():
        pl.semaphore_wait(relay.at[0], 6)
        signal_relay(1, z=4)
        signal_relay(1, z=-4)

    def select():
        lax.fori_loop(0, npts // 128, select_chunk, 0)
        get_pool.wait()

    steps = {
        "first": spread_first, "second": spread_second, "take": take, "other": take_other,
        "select": select, "gather": gather_chunk, "group": group_work,
        "near": relay_near, "far": relay_far,
    }
    for name, *where in PLAN:
        steps[name](*where)
    pl.semaphore_wait(relay.at[1], 2)

    def grad_of(slot):
        part = slice(slot * 4 * ncen, (slot + 1) * 4 * ncen)
        return jnp.dot(kern[part, :], resb[...], preferred_element_type=F32)

    for i in range(4):
        gq[i] = grad_of(other[i])
        send(gq.at[i], gq_in.at[i], sgq.at[i], rgq.at[i], partner=True)
    total = []
    for i in range(4):
        mine = grad_of(own[i])
        arrived(gq_in.at[i], rgq.at[i])
        both = mine + gq_in[i]
        total.append(both[0:ncen])
        for j in (1, 2, 3):
            gs[j, i] = both[j * ncen : (j + 1) * ncen].astype(BF16)
        if i in (1, 3):
            part = slice(i - 1, i + 1)
            send(gs.at[3, part], gs_in.at[3, part], sgs.at[3, i], rgs.at[3], s=2 if i == 1 else -2)
            for j in (1, 2):
                send(gs.at[j, part], gs_in.at[NEG[j], part], sgs.at[j, i], rgs.at[NEG[j]], s=OFFS[j])
    for j in (1, 2, 3):
        arrived(gs_in.at[j], rgs.at[j])
    eighth = ncen // NX
    for i in (3, 1, 2, 0):
        whole = total[i] + gs_in[1, i].astype(F32) + gs_in[2, i].astype(F32) + gs_in[3, i].astype(F32)
        gf[i] = whole.reshape(NX, eighth, outs)
    for i in (3, 1, 2, 0):
        for k in (3, 1, 2, 0):
            if i or k:
                df, dx = fx_offset(i, k)
                piece = lax.rem(here[0] + (dx + NX), NX)
                send(gf.at[i, piece], gf_in.at[NEG[i], NEG[k]], sgf.at[i, k], rgf.at[NEG[i], NEG[k]], f=df, x=dx)
    mine = gf[0, here[0]]
    for i in range(4):
        for k in range(4):
            if i or k:
                arrived(gf_in.at[i, k], rgf.at[i, k])
                mine = mine + gf_in[i, k]

    gz[...] = mine
    for k, dz in enumerate((4, -4, 8)):
        send(gz, gz_in.at[k], sgz.at[k], rgz.at[k], z=dz)
    for k in range(3):
        arrived(gz_in.at[k], rgz.at[k])
    out[here[0]] = (mine + gz_in[0]) + (gz_in[1] + gz_in[2])
    for k in (3, 1, 2):
        send(out.at[here[0]], out.at[here[0]], sgx.at[k], rgx.at[NEG[k]], x=OFFS[k])
    for k in (1, 2, 3):
        arrived(out.at[lax.rem(here[0] + (OFFS[k] + NX), NX)], rgx.at[k])
    grad_ref[...] = out[...].reshape(grad_ref.shape)

    for copy in pending:
        copy.wait_send()


def per_device(point_pool, batch_rows, targets, center_pool, center_rows, coefs):
    batch_rows, center_rows = batch_rows.reshape(-1, 128), center_rows.reshape(1, -1)
    npool, d = point_pool.shape
    npts, outs = targets.shape
    ncen = coefs.shape[0]
    vmem = pl.BlockSpec(memory_space=pltpu.VMEM)
    anys = pl.BlockSpec(memory_space=pl.ANY)
    dma = pltpu.SemaphoreType.DMA
    half = 4 * ncen
    sub = ncen // NX
    scratch = [
        pltpu.VMEM((8, 4, ncen, d + outs), BF16),
        pltpu.VMEM((npool, d), BF16),
        pltpu.VMEM((npts, npool), BF16),
        pltpu.VMEM((npts, d), BF16),
        pltpu.VMEM((npts, 1), F32),
        pltpu.VMEM((npts, 32 * ncen), BF16),
        pltpu.VMEM((npts, outs), BF16),
        pltpu.VMEM((npts, outs), BF16),
        pltpu.VMEM(center_pool.shape, BF16),
        pltpu.VMEM((npts // 128, 128), jnp.int32),
        pltpu.VMEM((1, ncen), jnp.int32),
        pltpu.VMEM((4, half, outs), F32),
        pltpu.VMEM((4, half, outs), F32),
        pltpu.VMEM((4, 4, ncen, outs), BF16),
        pltpu.VMEM((4, 4, ncen, outs), BF16),
        pltpu.VMEM((4, NX, sub, outs), F32),
        pltpu.VMEM((4, NX, sub, outs), F32),
        pltpu.VMEM((sub, outs), F32),
        pltpu.VMEM((3, sub, outs), F32),
        pltpu.VMEM((NX, sub, outs), F32),
        dma((6,)), dma((4,)), dma((4, 4)), dma((4, 4)), dma((4, 4)), dma((4, 4)),
        dma((4,)), dma((4,)), dma((4, 4)), dma((4,)), dma((4, 4)), dma((4, 4)),
        dma((3,)), dma((3,)), dma((4,)), dma((4,)), pltpu.SemaphoreType.REGULAR((2,)),
    ]
    return pl.pallas_call(
        kernel,
        out_shape=(
            jax.ShapeDtypeStruct((npts, outs), F32),
            jax.ShapeDtypeStruct((ncen, outs), F32),
        ),
        in_specs=[anys] * 6,
        out_specs=(vmem, vmem),
        scratch_shapes=scratch,
        compiler_params=pltpu.CompilerParams(
            collective_id=0, has_side_effects=True, vmem_limit_bytes=44 << 20
        ),
        name="regression",
    )(*(
        pltpu.with_memory_space_constraint(a, pltpu.HBM)
        for a in (point_pool, batch_rows, targets, center_pool, center_rows, coefs)
    ))


def solution(mesh):
    both = ("blk", "rep")
    in_specs = (P(both, None), P(both), P(both, None), P("blk", None), P("blk"), P("blk", None))
    out_specs = (P(both, None), P("blk", None))
    return jax.shard_map(per_device, mesh=mesh, in_specs=in_specs, out_specs=out_specs, check_vma=False)
```

```python
import functools

import jax
import jax.numpy as jnp
from jax import lax
from jax.experimental import pallas as pl
from jax.experimental.pallas import tpu as pltpu
from jax.sharding import PartitionSpec as P

MESH = pl.DeviceIdType.MESH
F32 = jnp.float32
BF16 = jnp.bfloat16
OFFS = (0, 1, -1, 2)
NEG = (0, 2, 1, 3)
NX, NY, NL, NH, NZ = 4, 4, 4, 4, 16
STEPS = 1
PLAN = (
    ("first",), ("take", 0, 0), ("near",), ("select",), ("second", 0),
    ("gather", 0), ("gather", 1),
    ("take", 1, 0), ("second", 1), ("take", 2, 0), ("second", 2),
    ("gather", 2),
    ("take", 3, 0), ("second", 3), ("take", 0, 1), ("take", 0, 2), ("take", 0, 3),
    ("gather", 3), ("far",), ("ready",), ("other", 0),
    ("group", 0),
    ("take", 1, 1), ("take", 1, 2), ("take", 2, 1), ("take", 2, 2), ("take", 1, 3), ("take", 2, 3),
    ("group", 1),
    ("take", 3, 1), ("take", 3, 2), ("take", 3, 3), ("other", 1), ("other", 2),
    ("group", 2),
    ("other", 3),
    ("group", 3),
)


def place():
    b = lax.axis_index("blk")
    r = lax.axis_index("rep")
    core = lax.rem(b, 2)
    z = lax.rem(r, NH) * NL + lax.rem(lax.div(b, 2), NL)
    return (lax.div(r, NH), lax.div(b, 2 * NL), z, core)


def at(here, f=0, s=0, x=0, z=0, partner=False):
    px, py, pz, core = here
    nx = lax.rem(px + (x + NX), NX)
    ny = lax.rem(py + (1 - core) * f + core * s + NY, NY)
    nz = lax.rem(pz + core * f + (1 - core) * s + (z + NZ), NZ)
    nc = 1 - core if partner else core
    return {"blk": (ny * NL + lax.rem(nz, NL)) * 2 + nc, "rep": nx * NH + lax.div(nz, NL)}


def fx_offset(i, j):
    df = OFFS[i]
    if df == 2 and j in (1, 2):
        df = -2
    return df, OFFS[j]


def destinations():
    out = [dict(partner=True)]
    for k in (1, -1, 2, -2):
        out += [dict(f=k), dict(s=k)]
    for k in (1, -1, 2):
        out.append(dict(x=k))
    return out


def opposite(offset):
    return {k: (v if k == "partner" else -v) for k, v in offset.items()}


def kernel(
    pool_hbm, rows_hbm, targ_hbm, cpool_hbm, crows_hbm, coefs_hbm,
    res, grad_ref,
    cen, pool, sel, pts, pnorm, kern, resb, targ, cpool, rows_ref, crows_ref,
    gq, gq_in, gs, gs_in, gf, gf_in, gz, gz_in, out,
    lsem, send1, send2, send_c, recv_p, recv_q,
    sgq, rgq, sgs, rgs, sgf, rgf, sgz, rgz, sgx, rgx, relay,
):
    npts, d = pts.shape
    npool = pool.shape[0]
    ncen, outs = coefs_hbm.shape
    group = 8 * ncen
    half = ncen // 2

    get_crows = pltpu.make_async_copy(crows_hbm, crows_ref, lsem.at[1])
    get_cpool = pltpu.make_async_copy(cpool_hbm, cpool, lsem.at[2])
    get_coefs = pltpu.make_async_copy(coefs_hbm, cen.at[0, 0, :, pl.ds(d, outs)], lsem.at[3])
    get_rows = pltpu.make_async_copy(rows_hbm, rows_ref, lsem.at[4])
    get_pool = pltpu.make_async_copy(pool_hbm, pool, lsem.at[0])
    get_targ = pltpu.make_async_copy(targ_hbm, targ, lsem.at[5])
    for copy in (get_crows, get_cpool, get_coefs):
        copy.start()

    here = place()
    known = {}

    def device(**offset):
        key = tuple(sorted(offset.items()))
        if key not in known:
            known[key] = at(here, **offset)
        return known[key]

    barrier = pltpu.get_barrier_semaphore()
    dests = destinations()
    for offset in dests:
        pl.semaphore_signal(barrier, inc=1, device_id=device(**opposite(offset)), device_id_type=MESH)

    for copy in (get_rows, get_pool, get_targ):
        copy.start()

    pending = []

    def sent():
        for copy in pending:
            copy.wait_send()
        pending.clear()

    def send(src, dst, ssem, rsem, **offset):
        copy = pltpu.make_async_remote_copy(
            src_ref=src, dst_ref=dst, send_sem=ssem, recv_sem=rsem,
            device_id=device(**offset), device_id_type=MESH,
        )
        copy.start()
        pending.append(copy)

    def arrived(ref, rsem):
        pltpu.make_async_remote_copy(
            src_ref=ref, dst_ref=ref, send_sem=sgx.at[0], recv_sem=rsem,
            device_id=device(partner=True), device_id_type=MESH,
        ).wait_recv()

    get_crows.wait()
    get_cpool.wait()
    chosen = (
        lax.broadcasted_iota(jnp.int32, (cpool.shape[0], ncen), 0) == crows_ref[...]
    ).astype(F32).astype(BF16)
    cen[0, 0, :, 0:d] = lax.dot_general(
        chosen, cpool[...], (((0,), (0,)), ((), ())), preferred_element_type=F32
    ).astype(BF16)
    get_coefs.wait()

    def select_chunk(k, _):
        row = jnp.broadcast_to(rows_ref[pl.ds(k, 1), :].astype(F32), (128, 128))
        col = jnp.concatenate([row.T.astype(jnp.int32)] * (npool // 128), axis=1)
        hit = col == lax.broadcasted_iota(jnp.int32, (128, npool), 1)
        sel[pl.ds(pl.multiple_of(k * 128, 128), 128), :] = hit.astype(F32).astype(BF16)
        return 0

    pl.semaphore_wait(barrier, len(dests))

    def signal_relay(k, **offset):
        pl.semaphore_signal(relay.at[k], inc=1, device_id=device(**offset), device_id_type=MESH)

    own = (0, 2, 3, 6)
    other = (1, 4, 5, 7)
    row_of = {slot: k * 4 * ncen for k, slot in enumerate(own + other)}

    def spread_first():
        block = cen.at[0, 0]
        send(block.at[0:half], cen.at[own[3], 0, 0:half], send1.at[0], recv_p.at[3, 0], f=2)
        send(block.at[half:ncen], cen.at[own[3], 0, half:ncen], send1.at[3], recv_p.at[3, 0], f=-2)
        for i in (1, 2):
            send(block, cen.at[own[NEG[i]], 0], send1.at[i], recv_p.at[NEG[i], 0], f=OFFS[i])

    def spread_second(i):
        block = cen.at[own[i], 0]
        send(block.at[0:half], cen.at[own[i], 3, 0:half], send2.at[i, 0], recv_p.at[i, 3], s=2)
        send(block.at[half:ncen], cen.at[own[i], 3, half:ncen], send2.at[i, 3], recv_p.at[i, 3], s=-2)
        for j in (1, 2):
            send(block, cen.at[own[i], NEG[j]], send2.at[i, j], recv_p.at[i, NEG[j]], s=OFFS[j])

    def take(i, j):
        if i or j:
            arrived(cen.at[own[i], j], recv_p.at[i, j])
        send(cen.at[own[i], j], cen.at[other[i], j], send_c.at[i, j], recv_q.at[i, j], partner=True)

    def take_other(i):
        for j in range(4):
            arrived(cen.at[other[i], j], recv_q.at[i, j])

    def gather_chunk(n):
        cols = slice(n * 256, n * 256 + 256)
        got = jnp.dot(sel[...], pool[:, cols], preferred_element_type=F32)
        pts[:, cols] = got.astype(BF16)
        square = jnp.sum(got * got, axis=1, keepdims=True)
        if n == 0:
            pnorm[...] = square
        else:
            pnorm[...] += square

    def group_work(g):
        centers = cen[2 * g : 2 * g + 2, :, :, 0:d].reshape(group, d)
        weights = cen[2 * g : 2 * g + 2, :, :, d : d + outs].reshape(group, outs)
        square = centers.astype(F32)
        square = square * square
        part = square[:, 0:128]
        for t in range(1, d // 128):
            part = part + square[:, t * 128 : (t + 1) * 128]
        cnorm = jnp.sum(part.T, axis=0, keepdims=True)
        step = npts // STEPS

        def rows_work(r, _):
            rows = pl.ds(pl.multiple_of(r * step, step), step)
            inner = lax.dot_general(
                pts[rows, :], centers, (((1,), (1,)), ((), ())), preferred_element_type=F32
            )
            distance = pnorm[rows, :] + cnorm - 2.0 * inner
            block = jnp.exp(distance * (-1.0 / d)).astype(BF16)
            flipped = block.T
            for k in (2 * g, 2 * g + 1):
                at_row = row_of[k]
                kern[at_row : at_row + group // 2, rows] = flipped[(k % 2) * group // 2 : (k % 2 + 1) * group // 2]
            term = jnp.dot(block, weights, preferred_element_type=F32)
            if g == 0:
                res[rows, :] = term - targ[rows, :].astype(F32)
            elif g < 3:
                res[rows, :] += term
            else:
                last = res[rows, :] + term
                res[rows, :] = last
                resb[rows, :] = last.astype(BF16)
            return 0

        lax.fori_loop(0, STEPS, rows_work, 0)

    def relay_near():
        for k in (1, -1, 2, -2):
            signal_relay(0, f=k)
        for k in (2, -2):
            signal_relay(0, s=k)

    def relay_far():
        pl.semaphore_wait(relay.at[0], 6)
        signal_relay(1, z=4)
        signal_relay(1, z=-4)

    def select():
        get_rows.wait()
        lax.fori_loop(0, npts // 128, select_chunk, 0)
        get_pool.wait()

    steps = {
        "first": spread_first, "second": spread_second, "take": take, "other": take_other,
        "select": select, "gather": gather_chunk, "group": group_work,
        "near": relay_near, "far": relay_far,
    }
    def ready():
        for i in range(4):
            for k in range(4):
                if i or k:
                    df, dx = fx_offset(i, k)
                    device(f=df, x=dx)
        for dz in (4, -4, 8):
            device(z=dz)
        get_targ.wait()

    steps["ready"] = ready
    for name, *where in PLAN:
        steps[name](*where)
    pl.semaphore_wait(relay.at[1], 2)

    def grad_of(first):
        rows = slice(first * group, (first + 1) * group)
        both = jnp.dot(kern[rows, :], resb[...], preferred_element_type=F32)
        return both.reshape(2, 4, ncen, outs)

    for h in (0, 1):
        part = slice(2 * h, 2 * h + 2)
        gq[part] = grad_of(2 + h)
        send(gq.at[part], gq_in.at[part], sgq.at[h], rgq.at[h], partner=True)
    total = []
    for h in (0, 1):
        part = slice(2 * h, 2 * h + 2)
        mine = grad_of(h)
        arrived(gq_in.at[part], rgq.at[h])
        both = mine + gq_in[part]
        total += [both[0, 0], both[1, 0]]
        for j in (1, 2, 3):
            gs[j, part] = both[:, j].astype(BF16)
        send(gs.at[3, part], gs_in.at[3, part], sgs.at[3, h], rgs.at[3], s=-2 if h else 2)
        for j in (1, 2):
            send(gs.at[j, part], gs_in.at[NEG[j], part], sgs.at[j, h], rgs.at[NEG[j]], s=OFFS[j])
    sent()
    for j in (1, 2, 3):
        arrived(gs_in.at[j], rgs.at[j])
    eighth = ncen // NX
    for i in (3, 1, 2, 0):
        whole = total[i] + gs_in[1, i].astype(F32) + gs_in[2, i].astype(F32) + gs_in[3, i].astype(F32)
        gf[i] = whole.reshape(NX, eighth, outs)
    for i in (3, 1, 2, 0):
        for k in (3, 1, 2, 0):
            if i or k:
                df, dx = fx_offset(i, k)
                piece = lax.rem(here[0] + (dx + NX), NX)
                send(gf.at[i, piece], gf_in.at[NEG[i], NEG[k]], sgf.at[i, k], rgf.at[NEG[i], NEG[k]], f=df, x=dx)
    sent()
    mine = gf[0, here[0]]
    for i in range(4):
        for k in range(4):
            if i or k:
                arrived(gf_in.at[i, k], rgf.at[i, k])
                mine = mine + gf_in[i, k]

    gz[...] = mine
    for k, dz in enumerate((4, -4, 8)):
        send(gz, gz_in.at[k], sgz.at[k], rgz.at[k], z=dz)
    sent()
    for k in range(3):
        arrived(gz_in.at[k], rgz.at[k])
    out[here[0]] = (mine + gz_in[0]) + (gz_in[1] + gz_in[2])
    for k in (3, 1, 2):
        send(out.at[here[0]], out.at[here[0]], sgx.at[k], rgx.at[NEG[k]], x=OFFS[k])
    for k in (1, 2, 3):
        arrived(out.at[lax.rem(here[0] + (OFFS[k] + NX), NX)], rgx.at[k])
    grad_ref[...] = out[...].reshape(grad_ref.shape)

    sent()


def per_device(point_pool, batch_rows, targets, center_pool, center_rows, coefs):
    batch_rows, center_rows = batch_rows.reshape(-1, 128), center_rows.reshape(1, -1)
    npool, d = point_pool.shape
    npts, outs = targets.shape
    ncen = coefs.shape[0]
    vmem = pl.BlockSpec(memory_space=pltpu.VMEM)
    anys = pl.BlockSpec(memory_space=pl.ANY)
    dma = pltpu.SemaphoreType.DMA
    sub = ncen // NX
    scratch = [
        pltpu.VMEM((8, 4, ncen, d + outs), BF16),
        pltpu.VMEM((npool, d), BF16),
        pltpu.VMEM((npts, npool), BF16),
        pltpu.VMEM((npts, d), BF16),
        pltpu.VMEM((npts, 1), F32),
        pltpu.VMEM((npts, 32 * ncen), BF16),
        pltpu.VMEM((npts, outs), BF16),
        pltpu.VMEM((npts, outs), BF16),
        pltpu.VMEM(center_pool.shape, BF16),
        pltpu.VMEM((npts // 128, 128), jnp.int32),
        pltpu.VMEM((1, ncen), jnp.int32),
        pltpu.VMEM((4, 4, ncen, outs), F32),
        pltpu.VMEM((4, 4, ncen, outs), F32),
        pltpu.VMEM((4, 4, ncen, outs), BF16),
        pltpu.VMEM((4, 4, ncen, outs), BF16),
        pltpu.VMEM((4, NX, sub, outs), F32),
        pltpu.VMEM((4, NX, sub, outs), F32),
        pltpu.VMEM((sub, outs), F32),
        pltpu.VMEM((3, sub, outs), F32),
        pltpu.VMEM((NX, sub, outs), F32),
        dma((6,)), dma((4,)), dma((4, 4)), dma((4, 4)), dma((4, 4)), dma((4, 4)),
        dma((4,)), dma((4,)), dma((4, 4)), dma((4,)), dma((4, 4)), dma((4, 4)),
        dma((3,)), dma((3,)), dma((4,)), dma((4,)), pltpu.SemaphoreType.REGULAR((2,)),
    ]
    return pl.pallas_call(
        kernel,
        out_shape=(
            jax.ShapeDtypeStruct((npts, outs), F32),
            jax.ShapeDtypeStruct((ncen, outs), F32),
        ),
        in_specs=[anys] * 6,
        out_specs=(vmem, vmem),
        scratch_shapes=scratch,
        compiler_params=pltpu.CompilerParams(
            collective_id=0, has_side_effects=True, vmem_limit_bytes=44 << 20
        ),
        name="regression",
    )(*(
        pltpu.with_memory_space_constraint(a, pltpu.HBM)
        for a in (point_pool, batch_rows, targets, center_pool, center_rows, coefs)
    ))


def solution(mesh):
    both = ("blk", "rep")
    in_specs = (P(both, None), P(both), P(both, None), P("blk", None), P("blk"), P("blk", None))
    out_specs = (P(both, None), P("blk", None))
    return jax.shard_map(per_device, mesh=mesh, in_specs=in_specs, out_specs=out_specs, check_vma=False)
```

```python
import functools

import jax
import jax.numpy as jnp
from jax import lax
from jax.experimental import pallas as pl
from jax.experimental.pallas import tpu as pltpu
from jax.sharding import PartitionSpec as P

MESH = pl.DeviceIdType.MESH
F32 = jnp.float32
BF16 = jnp.bfloat16
OFFS = (0, 1, -1, 2)
NEG = (0, 2, 1, 3)
NX, NY, NL, NH, NZ = 4, 4, 4, 4, 16
STEPS = 1
PLAN = (
    ("first",), ("take", 0, 0), ("near",), ("select",), ("second", 0),
    ("gather", 0), ("gather", 1),
    ("take", 1, 0), ("second", 1), ("take", 2, 0), ("second", 2),
    ("gather", 2),
    ("take", 3, 0), ("second", 3), ("take", 0, 1), ("take", 0, 2), ("take", 0, 3),
    ("gather", 3), ("far",), ("ready",), ("other", 0),
    ("group", 0),
    ("take", 1, 1), ("take", 1, 2), ("take", 2, 1), ("take", 2, 2), ("take", 1, 3), ("take", 2, 3),
    ("group", 1),
    ("take", 3, 1), ("take", 3, 2), ("take", 3, 3), ("other", 1), ("other", 2),
    ("group", 2),
    ("other", 3),
    ("group", 3),
)


def place():
    b = lax.axis_index("blk")
    r = lax.axis_index("rep")
    core = lax.rem(b, 2)
    z = lax.rem(r, NH) * NL + lax.rem(lax.div(b, 2), NL)
    return (lax.div(r, NH), lax.div(b, 2 * NL), z, core)


def at(here, f=0, s=0, x=0, z=0, partner=False):
    px, py, pz, core = here
    nx = lax.rem(px + (x + NX), NX)
    ny = lax.rem(py + (1 - core) * f + core * s + NY, NY)
    nz = lax.rem(pz + core * f + (1 - core) * s + (z + NZ), NZ)
    nc = 1 - core if partner else core
    return {"blk": (ny * NL + lax.rem(nz, NL)) * 2 + nc, "rep": nx * NH + lax.div(nz, NL)}


def fx_offset(i, j):
    df = OFFS[i]
    if df == 2 and j in (1, 2):
        df = -2
    return df, OFFS[j]


def destinations():
    out = [dict(partner=True)]
    for k in (1, -1, 2, -2):
        out += [dict(f=k), dict(s=k)]
    for k in (1, -1, 2):
        out.append(dict(x=k))
    return out


def opposite(offset):
    return {k: (v if k == "partner" else -v) for k, v in offset.items()}


def kernel(
    pool_hbm, rows_hbm, targ_hbm, cpool_hbm, crows_hbm, coefs_hbm,
    res, grad_ref,
    cen, pool, sel, pts, pnorm, kern, resb, targ, cpool, rows_ref, crows_ref,
    gq, gq_in, gs, gs_in, gf, gf_in, gz, gz_in, out,
    lsem, send1, send2, send_c, recv_p, recv_q,
    sgq, rgq, sgs, rgs, sgf, rgf, sgz, rgz, sgx, rgx, relay,
):
    npts, d = pts.shape
    npool = pool.shape[0]
    ncen, outs = coefs_hbm.shape
    group = 8 * ncen
    half = ncen // 2

    get_crows = pltpu.make_async_copy(crows_hbm, crows_ref, lsem.at[1])
    get_cpool = pltpu.make_async_copy(cpool_hbm, cpool, lsem.at[2])
    get_coefs = pltpu.make_async_copy(coefs_hbm, cen.at[0, 0, :, pl.ds(d, outs)], lsem.at[3])
    get_rows = pltpu.make_async_copy(rows_hbm, rows_ref, lsem.at[4])
    get_pool = pltpu.make_async_copy(pool_hbm, pool, lsem.at[0])
    get_targ = pltpu.make_async_copy(targ_hbm, targ, lsem.at[5])
    for copy in (get_crows, get_cpool, get_coefs):
        copy.start()

    here = place()
    known = {}

    def device(**offset):
        key = tuple(sorted(offset.items()))
        if key not in known:
            known[key] = at(here, **offset)
        return known[key]

    barrier = pltpu.get_barrier_semaphore()
    dests = destinations()
    for offset in dests:
        pl.semaphore_signal(barrier, inc=1, device_id=device(**opposite(offset)), device_id_type=MESH)

    for copy in (get_rows, get_pool, get_targ):
        copy.start()

    pending = []

    def sent():
        for copy in pending:
            copy.wait_send()
        pending.clear()

    def send(src, dst, ssem, rsem, **offset):
        copy = pltpu.make_async_remote_copy(
            src_ref=src, dst_ref=dst, send_sem=ssem, recv_sem=rsem,
            device_id=device(**offset), device_id_type=MESH,
        )
        copy.start()
        pending.append(copy)

    def arrived(ref, rsem):
        pltpu.make_async_remote_copy(
            src_ref=ref, dst_ref=ref, send_sem=sgx.at[0], recv_sem=rsem,
            device_id=device(partner=True), device_id_type=MESH,
        ).wait_recv()

    get_crows.wait()
    get_cpool.wait()
    chosen = (
        lax.broadcasted_iota(jnp.int32, (cpool.shape[0], ncen), 0) == crows_ref[...]
    ).astype(F32).astype(BF16)
    cen[0, 0, :, 0:d] = lax.dot_general(
        chosen, cpool[...], (((0,), (0,)), ((), ())), preferred_element_type=F32
    ).astype(BF16)
    get_coefs.wait()

    def select_chunk(k, _):
        row = jnp.broadcast_to(rows_ref[pl.ds(k, 1), :].astype(F32), (128, 128))
        col = jnp.concatenate([row.T.astype(jnp.int32)] * (npool // 128), axis=1)
        hit = col == lax.broadcasted_iota(jnp.int32, (128, npool), 1)
        sel[pl.ds(pl.multiple_of(k * 128, 128), 128), :] = hit.astype(F32).astype(BF16)
        return 0

    pl.semaphore_wait(barrier, len(dests))

    def signal_relay(k, **offset):
        pl.semaphore_signal(relay.at[k], inc=1, device_id=device(**offset), device_id_type=MESH)

    own = (0, 2, 3, 6)
    other = (1, 4, 5, 7)
    row_of = {slot: k * 4 * ncen for k, slot in enumerate(own + other)}

    def spread_first():
        block = cen.at[0, 0]
        send(block.at[0:half], cen.at[own[3], 0, 0:half], send1.at[0], recv_p.at[3, 0], f=2)
        send(block.at[half:ncen], cen.at[own[3], 0, half:ncen], send1.at[3], recv_p.at[3, 0], f=-2)
        for i in (1, 2):
            send(block, cen.at[own[NEG[i]], 0], send1.at[i], recv_p.at[NEG[i], 0], f=OFFS[i])

    def spread_second(i):
        block = cen.at[own[i], 0]
        send(block.at[0:half], cen.at[own[i], 3, 0:half], send2.at[i, 0], recv_p.at[i, 3], s=2)
        send(block.at[half:ncen], cen.at[own[i], 3, half:ncen], send2.at[i, 3], recv_p.at[i, 3], s=-2)
        for j in (1, 2):
            send(block, cen.at[own[i], NEG[j]], send2.at[i, j], recv_p.at[i, NEG[j]], s=OFFS[j])

    def take(i, j):
        if i or j:
            arrived(cen.at[own[i], j], recv_p.at[i, j])
        send(cen.at[own[i], j], cen.at[other[i], j], send_c.at[i, j], recv_q.at[i, j], partner=True)

    def take_other(i):
        for j in range(4):
            arrived(cen.at[other[i], j], recv_q.at[i, j])

    def gather_chunk(n):
        cols = slice(n * 256, n * 256 + 256)
        got = jnp.dot(sel[...], pool[:, cols], preferred_element_type=F32)
        pts[:, cols] = got.astype(BF16)
        square = jnp.sum(got * got, axis=1, keepdims=True)
        if n == 0:
            pnorm[...] = square
        else:
            pnorm[...] += square

    def group_work(g):
        centers = cen[2 * g : 2 * g + 2, :, :, 0:d].reshape(group, d)
        weights = cen[2 * g : 2 * g + 2, :, :, d : d + outs].reshape(group, outs)
        square = centers.astype(F32)
        square = square * square
        part = square[:, 0:128]
        for t in range(1, d // 128):
            part = part + square[:, t * 128 : (t + 1) * 128]
        cnorm = jnp.sum(part.T, axis=0, keepdims=True)
        step = npts // STEPS

        def rows_work(r, _):
            rows = pl.ds(pl.multiple_of(r * step, step), step)
            inner = lax.dot_general(
                pts[rows, :], centers, (((1,), (1,)), ((), ())), preferred_element_type=F32
            )
            distance = pnorm[rows, :] + cnorm - 2.0 * inner
            block = jnp.exp(distance * (-1.0 / d)).astype(BF16)
            flipped = block.T
            for k in (2 * g, 2 * g + 1):
                at_row = row_of[k]
                kern[at_row : at_row + group // 2, rows] = flipped[(k % 2) * group // 2 : (k % 2 + 1) * group // 2]
            term = jnp.dot(block, weights, preferred_element_type=F32)
            if g == 0:
                res[rows, :] = term - targ[rows, :].astype(F32)
            elif g < 3:
                res[rows, :] += term
            else:
                last = res[rows, :] + term
                res[rows, :] = last
                resb[rows, :] = last.astype(BF16)
            return 0

        lax.fori_loop(0, STEPS, rows_work, 0)

    def relay_near():
        for k in (1, -1, 2, -2):
            signal_relay(0, f=k)
        for k in (2, -2):
            signal_relay(0, s=k)

    def relay_far():
        pl.semaphore_wait(relay.at[0], 6)
        signal_relay(1, z=4)
        signal_relay(1, z=-4)

    def select():
        get_rows.wait()
        lax.fori_loop(0, npts // 128, select_chunk, 0)
        get_pool.wait()

    steps = {
        "first": spread_first, "second": spread_second, "take": take, "other": take_other,
        "select": select, "gather": gather_chunk, "group": group_work,
        "near": relay_near, "far": relay_far,
    }
    def ready():
        for i in range(4):
            for k in range(4):
                if i or k:
                    df, dx = fx_offset(i, k)
                    device(f=df, x=dx)
        for dz in (4, -4, 8):
            device(z=dz)
        get_targ.wait()

    steps["ready"] = ready
    for name, *where in PLAN:
        steps[name](*where)
    pl.semaphore_wait(relay.at[1], 2)

    def grad_of(first):
        rows = slice(first * group, (first + 1) * group)
        both = jnp.dot(kern[rows, :], resb[...], preferred_element_type=F32)
        return both.reshape(2, 4, ncen, outs)

    for h in (0, 1):
        part = slice(2 * h, 2 * h + 2)
        gq[part] = grad_of(2 + h)
        send(gq.at[part], gq_in.at[part], sgq.at[h], rgq.at[h], partner=True)
    total = []
    for h in (0, 1):
        part = slice(2 * h, 2 * h + 2)
        mine = grad_of(h)
        arrived(gq_in.at[part], rgq.at[h])
        both = mine + gq_in[part]
        total += [both[0, 0], both[1, 0]]
        for j in (1, 2, 3):
            gs[j, part] = both[:, j].astype(BF16)
        send(gs.at[3, part], gs_in.at[3, part], sgs.at[3, h], rgs.at[3], s=-2 if h else 2)
        for j in (1, 2):
            send(gs.at[j, part], gs_in.at[NEG[j], part], sgs.at[j, h], rgs.at[NEG[j]], s=OFFS[j])
    sent()
    for j in (1, 2, 3):
        arrived(gs_in.at[j], rgs.at[j])
    eighth = ncen // NX
    for i in (3, 1, 2, 0):
        whole = total[i] + gs_in[1, i].astype(F32) + gs_in[2, i].astype(F32) + gs_in[3, i].astype(F32)
        gf[i] = whole.reshape(NX, eighth, outs)
    for i in (3, 1, 2, 0):
        for k in (3, 1, 2, 0):
            if i or k:
                df, dx = fx_offset(i, k)
                piece = lax.rem(here[0] + (dx + NX), NX)
                send(gf.at[i, piece], gf_in.at[NEG[i], NEG[k]], sgf.at[i, k], rgf.at[NEG[i], NEG[k]], f=df, x=dx)
    sent()
    mine = gf[0, here[0]]
    for i in range(4):
        for k in range(4):
            if i or k:
                arrived(gf_in.at[i, k], rgf.at[i, k])
                mine = mine + gf_in[i, k]

    gz[...] = mine
    for k, dz in enumerate((4, -4, 8)):
        send(gz, gz_in.at[k], sgz.at[k], rgz.at[k], z=dz)
    sent()
    for k in range(3):
        arrived(gz_in.at[k], rgz.at[k])
    out[here[0]] = (mine + gz_in[0]) + (gz_in[1] + gz_in[2])
    for k in (3, 1, 2):
        send(out.at[here[0]], out.at[here[0]], sgx.at[k], rgx.at[NEG[k]], x=OFFS[k])
    for k in (1, 2, 3):
        arrived(out.at[lax.rem(here[0] + (OFFS[k] + NX), NX)], rgx.at[k])
    grad_ref[...] = out[...].reshape(grad_ref.shape)

    sent()


def put(res, grad, res_out, grad_out, sem):
    copies = (
        pltpu.make_async_copy(res, res_out, sem.at[0]),
        pltpu.make_async_copy(grad, grad_out, sem.at[1]),
    )
    for copy in copies:
        copy.start()
    for copy in copies:
        copy.wait()


def per_device(point_pool, batch_rows, targets, center_pool, center_rows, coefs):
    batch_rows, center_rows = batch_rows.reshape(-1, 128), center_rows.reshape(1, -1)
    npool, d = point_pool.shape
    npts, outs = targets.shape
    ncen = coefs.shape[0]
    vmem = pl.BlockSpec(memory_space=pltpu.VMEM)
    anys = pl.BlockSpec(memory_space=pl.ANY)
    dma = pltpu.SemaphoreType.DMA
    sub = ncen // NX
    scratch = [
        pltpu.VMEM((8, 4, ncen, d + outs), BF16),
        pltpu.VMEM((npool, d), BF16),
        pltpu.VMEM((npts, npool), BF16),
        pltpu.VMEM((npts, d), BF16),
        pltpu.VMEM((npts, 1), F32),
        pltpu.VMEM((npts, 32 * ncen), BF16),
        pltpu.VMEM((npts, outs), BF16),
        pltpu.VMEM((npts, outs), BF16),
        pltpu.VMEM(center_pool.shape, BF16),
        pltpu.VMEM((npts // 128, 128), jnp.int32),
        pltpu.VMEM((1, ncen), jnp.int32),
        pltpu.VMEM((4, 4, ncen, outs), F32),
        pltpu.VMEM((4, 4, ncen, outs), F32),
        pltpu.VMEM((4, 4, ncen, outs), BF16),
        pltpu.VMEM((4, 4, ncen, outs), BF16),
        pltpu.VMEM((4, NX, sub, outs), F32),
        pltpu.VMEM((4, NX, sub, outs), F32),
        pltpu.VMEM((sub, outs), F32),
        pltpu.VMEM((3, sub, outs), F32),
        pltpu.VMEM((NX, sub, outs), F32),
        dma((6,)), dma((4,)), dma((4, 4)), dma((4, 4)), dma((4, 4)), dma((4, 4)),
        dma((4,)), dma((4,)), dma((4, 4)), dma((4,)), dma((4, 4)), dma((4, 4)),
        dma((3,)), dma((3,)), dma((4,)), dma((4,)), pltpu.SemaphoreType.REGULAR((2,)),
    ]
    held = pl.pallas_call(
        kernel,
        out_shape=(
            jax.ShapeDtypeStruct((npts, outs), F32),
            jax.ShapeDtypeStruct((ncen, outs), F32),
        ),
        in_specs=[anys] * 6,
        out_specs=(vmem, vmem),
        scratch_shapes=scratch,
        compiler_params=pltpu.CompilerParams(
            collective_id=0, has_side_effects=True, vmem_limit_bytes=44 << 20
        ),
        name="regression",
    )(*(
        pltpu.with_memory_space_constraint(a, pltpu.HBM)
        for a in (point_pool, batch_rows, targets, center_pool, center_rows, coefs)
    ))
    return pl.pallas_call(
        put,
        out_shape=tuple(jax.ShapeDtypeStruct(a.shape, a.dtype) for a in held),
        in_specs=[anys] * 2,
        out_specs=(anys, anys),
        scratch_shapes=[dma((2,))],
        compiler_params=pltpu.CompilerParams(vmem_limit_bytes=1 << 20),
        name="put",
    )(*held)


def solution(mesh):
    both = ("blk", "rep")
    in_specs = (P(both, None), P(both), P(both, None), P("blk", None), P("blk"), P("blk", None))
    out_specs = (P(both, None), P("blk", None))
    return jax.shard_map(per_device, mesh=mesh, in_specs=in_specs, out_specs=out_specs, check_vma=False)
```

```python
import functools

import jax
import jax.numpy as jnp
from jax import lax
from jax.experimental import pallas as pl
from jax.experimental.pallas import tpu as pltpu
from jax.sharding import PartitionSpec as P

MESH = pl.DeviceIdType.MESH
F32 = jnp.float32
BF16 = jnp.bfloat16
OFFS = (0, 1, -1, 2)
NEG = (0, 2, 1, 3)
NX, NY, NL, NH, NZ = 4, 4, 4, 4, 16
STEPS = 1
PLAN = (
    ("first",), ("take", 0, 0), ("near",), ("select",), ("second", 0),
    ("gather", 0), ("gather", 1),
    ("take", 1, 0), ("second", 1), ("take", 2, 0), ("second", 2),
    ("gather", 2),
    ("take", 3, 0), ("second", 3), ("take", 0, 1), ("take", 0, 2), ("take", 0, 3),
    ("gather", 3), ("far",), ("ready",), ("other", 0),
    ("group", 0),
    ("take", 1, 1), ("take", 1, 2), ("take", 2, 1), ("take", 2, 2), ("take", 1, 3), ("take", 2, 3),
    ("group", 1),
    ("take", 3, 1), ("take", 3, 2), ("take", 3, 3), ("other", 1), ("other", 2),
    ("group", 2),
    ("other", 3),
    ("group", 3),
)


def place():
    b = lax.axis_index("blk")
    r = lax.axis_index("rep")
    core = lax.rem(b, 2)
    z = lax.rem(r, NH) * NL + lax.rem(lax.div(b, 2), NL)
    return (lax.div(r, NH), lax.div(b, 2 * NL), z, core)


def at(here, f=0, s=0, x=0, z=0, partner=False):
    px, py, pz, core = here
    nx = lax.rem(px + (x + NX), NX)
    ny = lax.rem(py + (1 - core) * f + core * s + NY, NY)
    nz = lax.rem(pz + core * f + (1 - core) * s + (z + NZ), NZ)
    nc = 1 - core if partner else core
    return {"blk": (ny * NL + lax.rem(nz, NL)) * 2 + nc, "rep": nx * NH + lax.div(nz, NL)}


def fx_offset(i, j):
    df = OFFS[i]
    if df == 2 and j in (1, 2):
        df = -2
    return df, OFFS[j]


def destinations():
    out = [dict(partner=True)]
    for k in (1, -1, 2, -2):
        out += [dict(f=k), dict(s=k)]
    for k in (1, -1, 2):
        out.append(dict(x=k))
    return out


def opposite(offset):
    return {k: (v if k == "partner" else -v) for k, v in offset.items()}


def kernel(
    pool_hbm, rows_hbm, targ_hbm, cpool_hbm, crows_hbm, coefs_hbm,
    res, grad_ref,
    cen, pool, sel, pts, pnorm, kern, resb, targ, cpool, rows_ref, crows_ref,
    gq, gq_in, gs, gs_in, gf, gf_in, gz, gz_in, out,
    lsem, send1, send2, send_c, recv_p, recv_q,
    sgq, rgq, sgs, rgs, sgf, rgf, sgz, rgz, sgx, rgx, relay,
):
    npts, d = pts.shape
    npool = pool.shape[0]
    ncen, outs = coefs_hbm.shape
    group = 8 * ncen
    half = ncen // 2

    get_crows = pltpu.make_async_copy(crows_hbm, crows_ref, lsem.at[1])
    get_cpool = pltpu.make_async_copy(cpool_hbm, cpool, lsem.at[2])
    get_coefs = pltpu.make_async_copy(coefs_hbm, cen.at[0, 0, :, pl.ds(d, outs)], lsem.at[3])
    get_rows = pltpu.make_async_copy(rows_hbm, rows_ref, lsem.at[4])
    get_pool = pltpu.make_async_copy(pool_hbm, pool, lsem.at[0])
    get_targ = pltpu.make_async_copy(targ_hbm, targ, lsem.at[5])
    for copy in (get_crows, get_cpool, get_coefs):
        copy.start()

    here = place()
    known = {}

    def device(**offset):
        key = tuple(sorted(offset.items()))
        if key not in known:
            known[key] = at(here, **offset)
        return known[key]

    barrier = pltpu.get_barrier_semaphore()
    dests = destinations()
    for offset in dests:
        pl.semaphore_signal(barrier, inc=1, device_id=device(**opposite(offset)), device_id_type=MESH)

    for copy in (get_rows, get_pool, get_targ):
        copy.start()

    pending = []

    def sent():
        for copy in pending:
            copy.wait_send()
        pending.clear()

    def send(src, dst, ssem, rsem, **offset):
        copy = pltpu.make_async_remote_copy(
            src_ref=src, dst_ref=dst, send_sem=ssem, recv_sem=rsem,
            device_id=device(**offset), device_id_type=MESH,
        )
        copy.start()
        pending.append(copy)

    def arrived(ref, rsem):
        pltpu.make_async_remote_copy(
            src_ref=ref, dst_ref=ref, send_sem=sgx.at[0], recv_sem=rsem,
            device_id=device(partner=True), device_id_type=MESH,
        ).wait_recv()

    get_crows.wait()
    get_cpool.wait()
    chosen = (
        lax.broadcasted_iota(jnp.int32, (cpool.shape[0], ncen), 0) == crows_ref[...]
    ).astype(F32).astype(BF16)
    cen[0, 0, :, 0:d] = lax.dot_general(
        chosen, cpool[...], (((0,), (0,)), ((), ())), preferred_element_type=F32
    ).astype(BF16)
    get_coefs.wait()

    def select_chunk(k, _):
        row = jnp.broadcast_to(rows_ref[pl.ds(k, 1), :].astype(F32), (128, 128))
        col = jnp.concatenate([row.T.astype(jnp.int32)] * (npool // 128), axis=1)
        hit = col == lax.broadcasted_iota(jnp.int32, (128, npool), 1)
        sel[pl.ds(pl.multiple_of(k * 128, 128), 128), :] = hit.astype(F32).astype(BF16)
        return 0

    pl.semaphore_wait(barrier, len(dests))

    def signal_relay(k, **offset):
        pl.semaphore_signal(relay.at[k], inc=1, device_id=device(**offset), device_id_type=MESH)

    own = (0, 2, 3, 6)
    other = (1, 4, 5, 7)
    row_of = {slot: k * 4 * ncen for k, slot in enumerate(own + other)}

    def spread_first():
        block = cen.at[0, 0]
        send(block.at[0:half], cen.at[own[3], 0, 0:half], send1.at[0], recv_p.at[3, 0], f=2)
        send(block.at[half:ncen], cen.at[own[3], 0, half:ncen], send1.at[3], recv_p.at[3, 0], f=-2)
        for i in (1, 2):
            send(block, cen.at[own[NEG[i]], 0], send1.at[i], recv_p.at[NEG[i], 0], f=OFFS[i])

    def spread_second(i):
        block = cen.at[own[i], 0]
        send(block.at[0:half], cen.at[own[i], 3, 0:half], send2.at[i, 0], recv_p.at[i, 3], s=2)
        send(block.at[half:ncen], cen.at[own[i], 3, half:ncen], send2.at[i, 3], recv_p.at[i, 3], s=-2)
        for j in (1, 2):
            send(block, cen.at[own[i], NEG[j]], send2.at[i, j], recv_p.at[i, NEG[j]], s=OFFS[j])

    def take(i, j):
        if i or j:
            arrived(cen.at[own[i], j], recv_p.at[i, j])
        send(cen.at[own[i], j], cen.at[other[i], j], send_c.at[i, j], recv_q.at[i, j], partner=True)

    def take_other(i):
        for j in range(4):
            arrived(cen.at[other[i], j], recv_q.at[i, j])

    def gather_chunk(n):
        cols = slice(n * 256, n * 256 + 256)
        got = jnp.dot(sel[...], pool[:, cols], preferred_element_type=F32)
        pts[:, cols] = got.astype(BF16)
        square = jnp.sum(got * got, axis=1, keepdims=True)
        if n == 0:
            pnorm[...] = square
        else:
            pnorm[...] += square

    def group_work(g):
        centers = cen[2 * g : 2 * g + 2, :, :, 0:d].reshape(group, d)
        weights = cen[2 * g : 2 * g + 2, :, :, d : d + outs].reshape(group, outs)
        square = centers.astype(F32)
        square = square * square
        part = square[:, 0:128]
        for t in range(1, d // 128):
            part = part + square[:, t * 128 : (t + 1) * 128]
        cnorm = jnp.sum(part.T, axis=0, keepdims=True)
        step = npts // STEPS

        def rows_work(r, _):
            rows = pl.ds(pl.multiple_of(r * step, step), step)
            inner = lax.dot_general(
                pts[rows, :], centers, (((1,), (1,)), ((), ())), preferred_element_type=F32
            )
            distance = pnorm[rows, :] + cnorm - 2.0 * inner
            block = jnp.exp(distance * (-1.0 / d)).astype(BF16)
            flipped = block.T
            for k in (2 * g, 2 * g + 1):
                at_row = row_of[k]
                kern[at_row : at_row + group // 2, rows] = flipped[(k % 2) * group // 2 : (k % 2 + 1) * group // 2]
            term = jnp.dot(block, weights, preferred_element_type=F32)
            if g == 0:
                res[rows, :] = term - targ[rows, :].astype(F32)
            elif g < 3:
                res[rows, :] += term
            else:
                last = res[rows, :] + term
                res[rows, :] = last
                resb[rows, :] = last.astype(BF16)
            return 0

        lax.fori_loop(0, STEPS, rows_work, 0)

    def relay_near():
        for k in (1, -1, 2, -2):
            signal_relay(0, f=k)
        for k in (2, -2):
            signal_relay(0, s=k)

    def relay_far():
        pl.semaphore_wait(relay.at[0], 6)
        signal_relay(1, z=4)
        signal_relay(1, z=-4)

    def select():
        get_rows.wait()
        lax.fori_loop(0, npts // 128, select_chunk, 0)
        get_pool.wait()

    steps = {
        "first": spread_first, "second": spread_second, "take": take, "other": take_other,
        "select": select, "gather": gather_chunk, "group": group_work,
        "near": relay_near, "far": relay_far,
    }
    def ready():
        for i in range(4):
            for k in range(4):
                if i or k:
                    df, dx = fx_offset(i, k)
                    device(f=df, x=dx)
        for dz in (4, -4, 8):
            device(z=dz)
        get_targ.wait()

    steps["ready"] = ready
    for name, *where in PLAN:
        steps[name](*where)
    pl.semaphore_wait(relay.at[1], 2)

    def grad_of(first):
        rows = slice(first * group, (first + 1) * group)
        both = jnp.dot(kern[rows, :], resb[...], preferred_element_type=F32)
        return both.reshape(2, 4, ncen, outs)

    for h in (0, 1):
        part = slice(2 * h, 2 * h + 2)
        gq[part] = grad_of(2 + h).astype(BF16)
        send(gq.at[part], gq_in.at[part], sgq.at[h], rgq.at[h], partner=True)
    total = []
    for h in (0, 1):
        part = slice(2 * h, 2 * h + 2)
        mine = grad_of(h)
        arrived(gq_in.at[part], rgq.at[h])
        both = mine + gq_in[part].astype(F32)
        total += [both[0, 0], both[1, 0]]
        for j in (1, 2, 3):
            gs[j, part] = both[:, j].astype(BF16)
        send(gs.at[3, part], gs_in.at[3, part], sgs.at[3, h], rgs.at[3], s=-2 if h else 2)
        for j in (1, 2):
            send(gs.at[j, part], gs_in.at[NEG[j], part], sgs.at[j, h], rgs.at[NEG[j]], s=OFFS[j])
    sent()
    for j in (1, 2, 3):
        arrived(gs_in.at[j], rgs.at[j])
    eighth = ncen // NX
    for i in (3, 1, 2, 0):
        whole = total[i] + gs_in[1, i].astype(F32) + gs_in[2, i].astype(F32) + gs_in[3, i].astype(F32)
        gf[i] = whole.reshape(NX, eighth, outs)
    for i in (3, 1, 2, 0):
        for k in (3, 1, 2, 0):
            if i or k:
                df, dx = fx_offset(i, k)
                piece = lax.rem(here[0] + (dx + NX), NX)
                send(gf.at[i, piece], gf_in.at[NEG[i], NEG[k]], sgf.at[i, k], rgf.at[NEG[i], NEG[k]], f=df, x=dx)
    sent()
    mine = gf[0, here[0]]
    for i in range(4):
        for k in range(4):
            if i or k:
                arrived(gf_in.at[i, k], rgf.at[i, k])
                mine = mine + gf_in[i, k]

    gz[...] = mine.astype(BF16)
    for k, dz in enumerate((4, -4, 8)):
        send(gz, gz_in.at[k], sgz.at[k], rgz.at[k], z=dz)
    sent()
    for k in range(3):
        arrived(gz_in.at[k], rgz.at[k])
    mine = gz[...].astype(F32)
    out[here[0]] = mine + (gz_in[0].astype(F32) + (gz_in[1].astype(F32) + gz_in[2].astype(F32)))
    for k in (3, 1, 2):
        send(out.at[here[0]], out.at[here[0]], sgx.at[k], rgx.at[NEG[k]], x=OFFS[k])
    for k in (1, 2, 3):
        arrived(out.at[lax.rem(here[0] + (OFFS[k] + NX), NX)], rgx.at[k])
    grad_ref[...] = out[...].reshape(grad_ref.shape)

    sent()


def put(res, grad, res_out, grad_out, sem):
    copies = (
        pltpu.make_async_copy(res, res_out, sem.at[0]),
        pltpu.make_async_copy(grad, grad_out, sem.at[1]),
    )
    for copy in copies:
        copy.start()
    for copy in copies:
        copy.wait()


def per_device(point_pool, batch_rows, targets, center_pool, center_rows, coefs):
    batch_rows, center_rows = batch_rows.reshape(-1, 128), center_rows.reshape(1, -1)
    npool, d = point_pool.shape
    npts, outs = targets.shape
    ncen = coefs.shape[0]
    vmem = pl.BlockSpec(memory_space=pltpu.VMEM)
    anys = pl.BlockSpec(memory_space=pl.ANY)
    dma = pltpu.SemaphoreType.DMA
    sub = ncen // NX
    scratch = [
        pltpu.VMEM((8, 4, ncen, d + outs), BF16),
        pltpu.VMEM((npool, d), BF16),
        pltpu.VMEM((npts, npool), BF16),
        pltpu.VMEM((npts, d), BF16),
        pltpu.VMEM((npts, 1), F32),
        pltpu.VMEM((npts, 32 * ncen), BF16),
        pltpu.VMEM((npts, outs), BF16),
        pltpu.VMEM((npts, outs), BF16),
        pltpu.VMEM(center_pool.shape, BF16),
        pltpu.VMEM((npts // 128, 128), jnp.int32),
        pltpu.VMEM((1, ncen), jnp.int32),
        pltpu.VMEM((4, 4, ncen, outs), BF16),
        pltpu.VMEM((4, 4, ncen, outs), BF16),
        pltpu.VMEM((4, 4, ncen, outs), BF16),
        pltpu.VMEM((4, 4, ncen, outs), BF16),
        pltpu.VMEM((4, NX, sub, outs), F32),
        pltpu.VMEM((4, NX, sub, outs), F32),
        pltpu.VMEM((sub, outs), BF16),
        pltpu.VMEM((3, sub, outs), BF16),
        pltpu.VMEM((NX, sub, outs), F32),
        dma((6,)), dma((4,)), dma((4, 4)), dma((4, 4)), dma((4, 4)), dma((4, 4)),
        dma((4,)), dma((4,)), dma((4, 4)), dma((4,)), dma((4, 4)), dma((4, 4)),
        dma((3,)), dma((3,)), dma((4,)), dma((4,)), pltpu.SemaphoreType.REGULAR((2,)),
    ]
    held = pl.pallas_call(
        kernel,
        out_shape=(
            jax.ShapeDtypeStruct((npts, outs), F32),
            jax.ShapeDtypeStruct((ncen, outs), F32),
        ),
        in_specs=[anys] * 6,
        out_specs=(vmem, vmem),
        scratch_shapes=scratch,
        compiler_params=pltpu.CompilerParams(
            collective_id=0, has_side_effects=True, vmem_limit_bytes=44 << 20
        ),
        name="regression",
    )(*(
        pltpu.with_memory_space_constraint(a, pltpu.HBM)
        for a in (point_pool, batch_rows, targets, center_pool, center_rows, coefs)
    ))
    return pl.pallas_call(
        put,
        out_shape=tuple(jax.ShapeDtypeStruct(a.shape, a.dtype) for a in held),
        in_specs=[anys] * 2,
        out_specs=(anys, anys),
        scratch_shapes=[dma((2,))],
        compiler_params=pltpu.CompilerParams(vmem_limit_bytes=1 << 20),
        name="put",
    )(*held)


def solution(mesh):
    both = ("blk", "rep")
    in_specs = (P(both, None), P(both), P(both, None), P("blk", None), P("blk"), P("blk", None))
    out_specs = (P(both, None), P("blk", None))
    return jax.shard_map(per_device, mesh=mesh, in_specs=in_specs, out_specs=out_specs, check_vma=False)
```

```python
import functools

import jax
import jax.numpy as jnp
from jax import lax
from jax.experimental import pallas as pl
from jax.experimental.pallas import tpu as pltpu
from jax.sharding import PartitionSpec as P

MESH = pl.DeviceIdType.MESH
F32 = jnp.float32
BF16 = jnp.bfloat16
OFFS = (0, 1, -1, 2)
NEG = (0, 2, 1, 3)
NX, NY, NL, NH, NZ = 4, 4, 4, 4, 16
STEPS = 1
PLAN = (
    ("first",), ("take", 0, 0), ("near",), ("select",), ("second", 0),
    ("gather", 0), ("gather", 1),
    ("take", 1, 0), ("second", 1), ("take", 2, 0), ("second", 2),
    ("gather", 2),
    ("take", 3, 0), ("second", 3), ("take", 0, 1), ("take", 0, 2), ("take", 0, 3),
    ("gather", 3), ("far",), ("ready",), ("other", 0),
    ("group", 0),
    ("take", 1, 1), ("take", 1, 2), ("take", 2, 1), ("take", 2, 2), ("take", 1, 3), ("take", 2, 3),
    ("group", 1),
    ("take", 3, 1), ("take", 3, 2), ("take", 3, 3), ("other", 1), ("other", 2),
    ("group", 2),
    ("other", 3),
    ("group", 3),
)


def place():
    b = lax.axis_index("blk")
    r = lax.axis_index("rep")
    core = lax.rem(b, 2)
    z = lax.rem(r, NH) * NL + lax.rem(lax.div(b, 2), NL)
    return (lax.div(r, NH), lax.div(b, 2 * NL), z, core)


def at(here, f=0, s=0, x=0, z=0, partner=False):
    px, py, pz, core = here
    nx = lax.rem(px + (x + NX), NX)
    ny = lax.rem(py + (1 - core) * f + core * s + NY, NY)
    nz = lax.rem(pz + core * f + (1 - core) * s + (z + NZ), NZ)
    nc = 1 - core if partner else core
    return {"blk": (ny * NL + lax.rem(nz, NL)) * 2 + nc, "rep": nx * NH + lax.div(nz, NL)}


def fx_offset(i, j):
    df = OFFS[i]
    if df == 2 and j in (1, 2):
        df = -2
    return df, OFFS[j]


def destinations():
    out = [dict(partner=True)]
    for k in (1, -1, 2, -2):
        out += [dict(f=k), dict(s=k)]
    for k in (1, -1, 2):
        out.append(dict(x=k))
    return out


def opposite(offset):
    return {k: (v if k == "partner" else -v) for k, v in offset.items()}


def kernel(
    pool_hbm, rows_hbm, targ_hbm, cpool_hbm, crows_hbm, coefs_hbm,
    res, grad_ref,
    cen, pool, sel, pts, pnorm, kern, resb, targ, cpool, rows_ref, crows_ref,
    gq, gq_in, gs, gs_in, gf, gf_in, gz, gz_in, out,
    lsem, send1, send2, send_c, recv_p, recv_q,
    sgq, rgq, sgs, rgs, sgf, rgf, sgz, rgz, sgx, rgx, relay,
):
    npts, d = pts.shape
    npool = pool.shape[0]
    ncen, outs = coefs_hbm.shape
    group = 8 * ncen
    half = ncen // 2

    get_crows = pltpu.make_async_copy(crows_hbm, crows_ref, lsem.at[1])
    get_cpool = pltpu.make_async_copy(cpool_hbm, cpool, lsem.at[2])
    get_coefs = pltpu.make_async_copy(coefs_hbm, cen.at[0, 0, :, pl.ds(d, outs)], lsem.at[3])
    get_rows = pltpu.make_async_copy(rows_hbm, rows_ref, lsem.at[4])
    get_pool = pltpu.make_async_copy(pool_hbm, pool, lsem.at[0])
    get_targ = pltpu.make_async_copy(targ_hbm, targ, lsem.at[5])
    for copy in (get_crows, get_cpool, get_coefs):
        copy.start()

    here = place()
    known = {}

    def device(**offset):
        key = tuple(sorted(offset.items()))
        if key not in known:
            known[key] = at(here, **offset)
        return known[key]

    barrier = pltpu.get_barrier_semaphore()
    dests = destinations()
    for offset in dests:
        pl.semaphore_signal(barrier, inc=1, device_id=device(**opposite(offset)), device_id_type=MESH)

    for copy in (get_rows, get_pool, get_targ):
        copy.start()

    pending = []

    def sent():
        for copy in pending:
            copy.wait_send()
        pending.clear()

    def send(src, dst, ssem, rsem, **offset):
        copy = pltpu.make_async_remote_copy(
            src_ref=src, dst_ref=dst, send_sem=ssem, recv_sem=rsem,
            device_id=device(**offset), device_id_type=MESH,
        )
        copy.start()
        pending.append(copy)

    def arrived(ref, rsem):
        pltpu.make_async_remote_copy(
            src_ref=ref, dst_ref=ref, send_sem=sgx.at[0], recv_sem=rsem,
            device_id=device(partner=True), device_id_type=MESH,
        ).wait_recv()

    get_crows.wait()
    get_cpool.wait()
    chosen = (
        lax.broadcasted_iota(jnp.int32, (cpool.shape[0], ncen), 0) == crows_ref[...]
    ).astype(F32).astype(BF16)
    cen[0, 0, :, 0:d] = lax.dot_general(
        chosen, cpool[...], (((0,), (0,)), ((), ())), preferred_element_type=F32
    ).astype(BF16)
    get_coefs.wait()

    def select_chunk(k, _):
        row = jnp.broadcast_to(rows_ref[pl.ds(k, 1), :].astype(F32), (128, 128))
        col = jnp.concatenate([row.T.astype(jnp.int32)] * (npool // 128), axis=1)
        hit = col == lax.broadcasted_iota(jnp.int32, (128, npool), 1)
        sel[pl.ds(pl.multiple_of(k * 128, 128), 128), :] = hit.astype(F32).astype(BF16)
        return 0

    pl.semaphore_wait(barrier, len(dests))

    def signal_relay(k, **offset):
        pl.semaphore_signal(relay.at[k], inc=1, device_id=device(**offset), device_id_type=MESH)

    own = (0, 2, 3, 6)
    other = (1, 4, 5, 7)
    row_of = {slot: k * 4 * ncen for k, slot in enumerate(own + other)}

    def spread_first():
        block = cen.at[0, 0]
        send(block.at[0:half], cen.at[own[3], 0, 0:half], send1.at[0], recv_p.at[3, 0], f=2)
        send(block.at[half:ncen], cen.at[own[3], 0, half:ncen], send1.at[3], recv_p.at[3, 0], f=-2)
        for i in (1, 2):
            send(block, cen.at[own[NEG[i]], 0], send1.at[i], recv_p.at[NEG[i], 0], f=OFFS[i])

    def spread_second(i):
        block = cen.at[own[i], 0]
        send(block.at[0:half], cen.at[own[i], 3, 0:half], send2.at[i, 0], recv_p.at[i, 3], s=2)
        send(block.at[half:ncen], cen.at[own[i], 3, half:ncen], send2.at[i, 3], recv_p.at[i, 3], s=-2)
        for j in (1, 2):
            send(block, cen.at[own[i], NEG[j]], send2.at[i, j], recv_p.at[i, NEG[j]], s=OFFS[j])

    def take(i, j):
        if i or j:
            arrived(cen.at[own[i], j], recv_p.at[i, j])
        send(cen.at[own[i], j], cen.at[other[i], j], send_c.at[i, j], recv_q.at[i, j], partner=True)

    def take_other(i):
        for j in range(4):
            arrived(cen.at[other[i], j], recv_q.at[i, j])

    def gather_chunk(n):
        cols = slice(n * 256, n * 256 + 256)
        got = jnp.dot(sel[...], pool[:, cols], preferred_element_type=F32)
        pts[:, cols] = got.astype(BF16)
        square = jnp.sum(got * got, axis=1, keepdims=True)
        if n == 0:
            pnorm[...] = square
        else:
            pnorm[...] += square

    def group_work(g):
        centers = cen[2 * g : 2 * g + 2, :, :, 0:d].reshape(group, d)
        weights = cen[2 * g : 2 * g + 2, :, :, d : d + outs].reshape(group, outs)
        square = centers.astype(F32)
        square = square * square
        part = square[:, 0:128]
        for t in range(1, d // 128):
            part = part + square[:, t * 128 : (t + 1) * 128]
        cnorm = jnp.sum(part.T, axis=0, keepdims=True)
        step = npts // STEPS

        def rows_work(r, _):
            rows = pl.ds(pl.multiple_of(r * step, step), step)
            inner = lax.dot_general(
                pts[rows, :], centers, (((1,), (1,)), ((), ())), preferred_element_type=F32
            )
            distance = pnorm[rows, :] + cnorm - 2.0 * inner
            block = jnp.exp(distance * (-1.0 / d)).astype(BF16)
            flipped = block.T
            for k in (2 * g, 2 * g + 1):
                at_row = row_of[k]
                kern[at_row : at_row + group // 2, rows] = flipped[(k % 2) * group // 2 : (k % 2 + 1) * group // 2]
            term = jnp.dot(block, weights, preferred_element_type=F32)
            if g == 0:
                res[rows, :] = term - targ[rows, :].astype(F32)
            elif g < 3:
                res[rows, :] += term
            else:
                last = res[rows, :] + term
                res[rows, :] = last
                resb[rows, :] = last.astype(BF16)
            return 0

        lax.fori_loop(0, STEPS, rows_work, 0)

    def relay_near():
        for k in (1, -1, 2, -2):
            signal_relay(0, f=k)
        for k in (2, -2):
            signal_relay(0, s=k)

    def relay_far():
        pl.semaphore_wait(relay.at[0], 6)
        signal_relay(1, z=4)
        signal_relay(1, z=-4)

    def select():
        get_rows.wait()
        lax.fori_loop(0, npts // 128, select_chunk, 0)
        get_pool.wait()

    steps = {
        "first": spread_first, "second": spread_second, "take": take, "other": take_other,
        "select": select, "gather": gather_chunk, "group": group_work,
        "near": relay_near, "far": relay_far,
    }
    def ready():
        for i in range(4):
            for k in range(4):
                if i or k:
                    df, dx = fx_offset(i, k)
                    device(f=df, x=dx)
        for dz in (4, -4, 8):
            device(z=dz)
        get_targ.wait()

    steps["ready"] = ready
    for name, *where in PLAN:
        steps[name](*where)
    pl.semaphore_wait(relay.at[1], 2)

    def grad_of(first):
        rows = slice(first * group, (first + 1) * group)
        both = jnp.dot(kern[rows, :], resb[...], preferred_element_type=F32)
        return both.reshape(2, 4, ncen, outs)

    for h in (0, 1):
        part = slice(2 * h, 2 * h + 2)
        gq[part] = grad_of(2 + h).astype(BF16)
        send(gq.at[part], gq_in.at[part], sgq.at[h], rgq.at[h], partner=True)
    total = []
    for h in (0, 1):
        part = slice(2 * h, 2 * h + 2)
        mine = grad_of(h)
        arrived(gq_in.at[part], rgq.at[h])
        both = mine + gq_in[part].astype(F32)
        total += [both[0, 0], both[1, 0]]
        for j in (1, 2, 3):
            gs[j, part] = both[:, j].astype(BF16)
        send(gs.at[3, part], gs_in.at[3, part], sgs.at[3, h], rgs.at[3], s=-2 if h else 2)
        for j in (1, 2):
            send(gs.at[j, part], gs_in.at[NEG[j], part], sgs.at[j, h], rgs.at[NEG[j]], s=OFFS[j])
    sent()
    for j in (1, 2, 3):
        arrived(gs_in.at[j], rgs.at[j])
    eighth = ncen // NX
    for i in (3, 1, 2, 0):
        whole = total[i] + gs_in[1, i].astype(F32) + gs_in[2, i].astype(F32) + gs_in[3, i].astype(F32)
        gf[i] = whole.reshape(NX, eighth, outs)
    for i in (3, 1, 2, 0):
        for k in (3, 1, 2, 0):
            if i or k:
                df, dx = fx_offset(i, k)
                piece = lax.rem(here[0] + (dx + NX), NX)
                send(gf.at[i, piece], gf_in.at[NEG[i], NEG[k]], sgf.at[i, k], rgf.at[NEG[i], NEG[k]], f=df, x=dx)
    sent()
    mine = gf[0, here[0]]
    for i in range(4):
        for k in range(4):
            if i or k:
                arrived(gf_in.at[i, k], rgf.at[i, k])
                mine = mine + gf_in[i, k]

    gz[...] = mine
    for k, dz in enumerate((4, -4, 8)):
        send(gz, gz_in.at[k], sgz.at[k], rgz.at[k], z=dz)
    sent()
    for k in range(3):
        arrived(gz_in.at[k], rgz.at[k])
    out[here[0]] = (mine + gz_in[0]) + (gz_in[1] + gz_in[2])
    for k in (3, 1, 2):
        send(out.at[here[0]], out.at[here[0]], sgx.at[k], rgx.at[NEG[k]], x=OFFS[k])
    for k in (1, 2, 3):
        arrived(out.at[lax.rem(here[0] + (OFFS[k] + NX), NX)], rgx.at[k])
    grad_ref[...] = out[...].reshape(grad_ref.shape)

    sent()


def put(res, grad, res_out, grad_out, sem):
    copies = (
        pltpu.make_async_copy(res, res_out, sem.at[0]),
        pltpu.make_async_copy(grad, grad_out, sem.at[1]),
    )
    for copy in copies:
        copy.start()
    for copy in copies:
        copy.wait()


def per_device(point_pool, batch_rows, targets, center_pool, center_rows, coefs):
    batch_rows, center_rows = batch_rows.reshape(-1, 128), center_rows.reshape(1, -1)
    npool, d = point_pool.shape
    npts, outs = targets.shape
    ncen = coefs.shape[0]
    vmem = pl.BlockSpec(memory_space=pltpu.VMEM)
    anys = pl.BlockSpec(memory_space=pl.ANY)
    dma = pltpu.SemaphoreType.DMA
    sub = ncen // NX
    scratch = [
        pltpu.VMEM((8, 4, ncen, d + outs), BF16),
        pltpu.VMEM((npool, d), BF16),
        pltpu.VMEM((npts, npool), BF16),
        pltpu.VMEM((npts, d), BF16),
        pltpu.VMEM((npts, 1), F32),
        pltpu.VMEM((npts, 32 * ncen), BF16),
        pltpu.VMEM((npts, outs), BF16),
        pltpu.VMEM((npts, outs), BF16),
        pltpu.VMEM(center_pool.shape, BF16),
        pltpu.VMEM((npts // 128, 128), jnp.int32),
        pltpu.VMEM((1, ncen), jnp.int32),
        pltpu.VMEM((4, 4, ncen, outs), BF16),
        pltpu.VMEM((4, 4, ncen, outs), BF16),
        pltpu.VMEM((4, 4, ncen, outs), BF16),
        pltpu.VMEM((4, 4, ncen, outs), BF16),
        pltpu.VMEM((4, NX, sub, outs), F32),
        pltpu.VMEM((4, NX, sub, outs), F32),
        pltpu.VMEM((sub, outs), F32),
        pltpu.VMEM((3, sub, outs), F32),
        pltpu.VMEM((NX, sub, outs), F32),
        dma((6,)), dma((4,)), dma((4, 4)), dma((4, 4)), dma((4, 4)), dma((4, 4)),
        dma((4,)), dma((4,)), dma((4, 4)), dma((4,)), dma((4, 4)), dma((4, 4)),
        dma((3,)), dma((3,)), dma((4,)), dma((4,)), pltpu.SemaphoreType.REGULAR((2,)),
    ]
    held = pl.pallas_call(
        kernel,
        out_shape=(
            jax.ShapeDtypeStruct((npts, outs), F32),
            jax.ShapeDtypeStruct((ncen, outs), F32),
        ),
        in_specs=[anys] * 6,
        out_specs=(vmem, vmem),
        scratch_shapes=scratch,
        compiler_params=pltpu.CompilerParams(
            collective_id=0, has_side_effects=True, vmem_limit_bytes=44 << 20
        ),
        name="regression",
    )(*(
        pltpu.with_memory_space_constraint(a, pltpu.HBM)
        for a in (point_pool, batch_rows, targets, center_pool, center_rows, coefs)
    ))
    return pl.pallas_call(
        put,
        out_shape=tuple(jax.ShapeDtypeStruct(a.shape, a.dtype) for a in held),
        in_specs=[anys] * 2,
        out_specs=(anys, anys),
        scratch_shapes=[dma((2,))],
        compiler_params=pltpu.CompilerParams(vmem_limit_bytes=1 << 20),
        name="put",
    )(*held)


def solution(mesh):
    both = ("blk", "rep")
    in_specs = (P(both, None), P(both), P(both, None), P("blk", None), P("blk"), P("blk", None))
    out_specs = (P(both, None), P("blk", None))
    return jax.shard_map(per_device, mesh=mesh, in_specs=in_specs, out_specs=out_specs, check_vma=False)
```
